128 devices in a mesh: sec: 2 (over y_hi), dev: 32 (over z, x, core), tp: 2 (over y_lo).
Axes of the slice: x: 4, y: 4 (y_hi: 2, y_lo: 2; y = y_hi * 2 + y_lo), z: 4, core: 2. Of those that a mesh axis runs over, the one named last changes fastest.
Arguments:
- queries: bfloat16 [512, 8192], P(('sec', 'dev'), 'tp'), may hold values from -6 to 6
- new_keys: bfloat16 [512, 1024], P(('sec', 'dev'), 'tp'), may hold values from -6 to 6
- token_values: bfloat16 [512, 1024], P(('sec', 'dev'), 'tp'), may hold values from -6 to 6
- key_cache: bfloat16 [512, 256, 1024], P(('sec', 'dev'), None, 'tp'), may hold values from -6 to 6
- stored_values: bfloat16 [512, 256, 1024], P(('sec', 'dev'), None, 'tp'), may hold values from -6 to 6
- cache_lengths: int32 [512], P(('sec', 'dev')), may hold values from 1 to 256, 65536 in all
- residual: bfloat16 [512, 8192], P(('sec', 'dev', 'tp')), may hold values from -6 to 6
- norm_gain: float32 [8192], replicated, may hold values from 0.25 to 1.75
- active: int32 [512, 16], P(('sec', 'dev', 'tp')), may hold values from 0 to 127, all different within a row; in each aligned block of 4 rows (0 to 3, 4 to 7, ...) at most 3 rows name the same one
- gate_weight: bfloat16 [8192, 16384], P(None, ('sec', 'dev', 'tp')), may hold values from -0.0625 to 0.0625
- up_weight: bfloat16 [8192, 16384], P(None, ('sec', 'dev', 'tp')), may hold values from -0.0625 to 0.0625
- down_weight: bfloat16 [16384, 8192], P(('sec', 'dev', 'tp')), may hold values from -0.125 to 0.125
Outputs:
- layer_out: bfloat16 [512, 8192], P(('sec', 'dev', 'tp'))
The draws below stay inside these ranges and needn't reach their ends.
Inputs may be any that keep to these rules, and one draw needn't show every extreme that they name: `cache_lengths`: the largest length is 256 in every draw. `active`: the bundles of one row are distinct. Among the 4 rows of one device (aligned blocks of rows), no bundle is named by more than 3 rows, and some bundle reaches 3.
All inputs are finite; a program needn't handle non-finite values. No bound on the sum of `cache_lengths` on one device may be relied on, other than what follows from the above.
Results may differ from the reference program's by a relative error of at most 0.007.
Values may be sent and summed in bfloat16 or wider, within the bound.
A program may use at most 128 MiB of HBM per device.

```python
import math
import jax
import jax.numpy as jnp
import numpy as np
from jax import lax

QUERY_HEADS = 64
VALUE_HEADS = 8
HEAD_SIZE = 128
BUNDLE = 128
TOP = 16
CACHE_POSITIONS = 256
D = 8192
REQUEST_TOTAL = 512
ROWS_DEV = 4
BUNDLES = 128
SLOT = 3


def draw_queries(key, part):
    sampled_draw = jnp.clip(jax.random.normal(jax.random.fold_in(key, 1), (REQUEST_TOTAL, QUERY_HEADS * HEAD_SIZE), jnp.float32), -6.0, 6.0)
    return sampled_draw.astype(jnp.bfloat16)


def draw_new_keys(key, part):
    sampled_draw = jnp.clip(jax.random.normal(jax.random.fold_in(key, 2), (REQUEST_TOTAL, VALUE_HEADS * HEAD_SIZE), jnp.float32), -6.0, 6.0)
    return sampled_draw.astype(jnp.bfloat16)


def draw_key_cache(key, part):
    sampled_draw = jnp.clip(jax.random.normal(jax.random.fold_in(key, 3), (REQUEST_TOTAL, CACHE_POSITIONS, VALUE_HEADS * HEAD_SIZE), jnp.float32), -6.0, 6.0)
    return sampled_draw.astype(jnp.bfloat16)


def block_scale(rng, extent, cuts, least, largest):
    loudness = 1.0
    for dim, parts in cuts:
        heights = jax.random.uniform(jax.random.fold_in(jax.random.fold_in(rng, 6), dim), (parts,), jnp.float32, least / len(cuts), largest / len(cuts))
        loudness = loudness * jnp.repeat(jnp.exp(heights), extent[dim] // parts).reshape((-1,) + (1,) * (len(extent) - 1 - dim))
    return loudness


def split_up(number_of, total, bound, skew):
    weights = [(1 << 20) // math.isqrt(standing ** skew) + 1 for standing in range(2, number_of + 1)]
    surplus, counts = total - bound - (number_of - 1), [1] * (number_of - 1)
    while surplus > 0:
        free = [i for i in range(number_of - 1) if counts[i] < bound]
        whole, budget = sum([weights[i] for i in free]), surplus
        for i in free:
            more = min(bound - counts[i], max(1, budget * weights[i] // whole), surplus)
            counts[i] = counts[i] + more
            surplus = surplus - more
    return np.array([bound] + counts)


def ragged(own_key, amount, total, reach, skew):
    if amount == 2:
        one = jax.random.randint(own_key, (), max(1, total - reach), min(reach, total - 1) + 1)
        return jnp.stack([one, total - one])
    tallies = jnp.asarray(split_up(amount, total, reach, skew), jnp.int32)
    couples = (amount - 1) // 2
    giver, taker = tallies[1:1 + 2 * couples:2], tallies[2:2 + 2 * couples:2]
    room = jnp.minimum(giver - 1, reach - taker)
    passed = jax.random.randint(jax.random.fold_in(own_key, 1), (couples,), 0, 1 << 20) % (room + 1)
    tallies = tallies.at[1:1 + 2 * couples:2].set(giver - passed).at[2:2 + 2 * couples:2].set(taker + passed)
    return tallies[jax.random.permutation(jax.random.fold_in(own_key, 2), amount)]


def deal_out(own_key, own, number, rows, count, top, most, slope):
    order = jax.random.permutation(own_key, count)
    crowded, usual = shares(count, rows * top, most, slope, True), shares(count, rows * top, most, slope, False)
    places = jnp.arange(count)

    def named(sizes, turn):
        used = int((sizes > 0).sum())
        fixed = max(1, used // 4)
        shifted = fixed + (places - fixed + turn * (used - fixed)) % max(1, count - fixed)
        return jnp.zeros((count,), jnp.int32).at[order[jnp.where(places < fixed, places, shifted)]].set(jnp.asarray(sizes, jnp.int32))

    sizes = jnp.where(number % 4 == 0, named(crowded, number // 4), named(usual, number - number // 4 - 1))
    mixed = jax.random.permutation(jax.random.fold_in(own, 3), count)
    giver, receiver = mixed[0:count // 2 * 2:2], mixed[1:count // 2 * 2:2]
    margin = jnp.minimum(sizes[giver] - 1, most - sizes[receiver]) // 2
    margin = jnp.where((giver == order[0]) | (receiver == order[0]) | (sizes[receiver] == 0), 0, jnp.maximum(margin, 0))
    shifted = jax.random.randint(jax.random.fold_in(own, 4), (count // 2,), 0, 1 << 20) % (margin + 1)
    sizes = sizes.at[giver].add(-shifted).at[receiver].add(shifted)
    members = jnp.searchsorted(jnp.cumsum(sizes), jnp.arange(rows * top), side="right").astype(jnp.int32)
    listing = members.reshape(top, rows).T
    listing = listing[jax.random.permutation(jax.random.fold_in(own, 1), rows)]
    turn = jax.random.randint(jax.random.fold_in(own, 2), (rows, 1), 0, top)
    return jnp.take_along_axis(listing, (jnp.arange(top)[None, :] + turn) % top, axis=1)


def shares(number_of, total, most, slope, full):
    loads = [(1 << 20) // math.isqrt(grade ** slope) + 1 for grade in range(1, number_of + 1)]
    largest = most if full else min(most, max(-(-total // number_of), total * loads[0] // sum(loads)))
    least = 1 if total - largest >= number_of - 1 else 0
    holding, spare = [largest] + [least] * (number_of - 1), total - largest - least * (number_of - 1)
    while spare > 0:
        movable = [i for i in range(1, number_of) if holding[i] < largest] or [i for i in range(1, number_of) if holding[i] < most]
        whole, left = sum([loads[i] for i in movable]), spare
        for i in movable:
            more = min(most - holding[i], max(1, left * loads[i] // whole), spare)
            holding[i] = holding[i] + more
            spare = spare - more
    return np.array(holding)


def centred(own_key, extent, scale, bound, pieces=(), held_as=jnp.bfloat16):
    drawn = jax.random.normal(own_key, extent, jnp.float32) * scale
    if len(pieces) > 0:
        drawn = block_scale(own_key, extent, pieces, -0.22, 0.18) * drawn
    return jnp.clip(drawn, min=-bound, max=bound).astype(held_as)


def setup_inputs(seed: int = 0) -> dict:
    key_list = jax.random.split(jax.random.key(seed), 13)
    queries = draw_queries(jax.random.fold_in(key_list[12], 71), 0)
    new_keys = draw_new_keys(jax.random.fold_in(key_list[12], 71), 0)
    token_values = centred(key_list[2], (REQUEST_TOTAL, VALUE_HEADS * HEAD_SIZE), 1.0, 6.0, ((0, 64), (1, 2)))
    key_cache = draw_key_cache(jax.random.fold_in(key_list[12], 71), 0)
    stored_values = centred(key_list[4], (REQUEST_TOTAL, CACHE_POSITIONS, VALUE_HEADS * HEAD_SIZE), 1.0, 6.0, ((0, 64), (2, 2)))
    cache_lengths = ragged(key_list[5], REQUEST_TOTAL, REQUEST_TOTAL * CACHE_POSITIONS // 2, CACHE_POSITIONS, 2).astype(jnp.int32)
    residual = centred(key_list[6], (REQUEST_TOTAL, D), 1.0, 6.0, ((0, 128),))
    norm_gain = jnp.clip(1.0 + 0.15 * jax.random.normal(key_list[7], (D,), jnp.float32), 0.25, 1.75)
    active_keys = jax.random.split(jax.random.fold_in(key_list[8], 1), REQUEST_TOTAL // ROWS_DEV)
    active_turns = jax.random.permutation(jax.random.fold_in(key_list[8], 3), REQUEST_TOTAL // ROWS_DEV)
    active = jax.vmap(lambda own, number: deal_out(jax.random.fold_in(key_list[8], 2), own, number, ROWS_DEV, BUNDLES, TOP, SLOT, 2))(active_keys, active_turns).reshape((REQUEST_TOTAL, TOP))
    gate_weight = centred(key_list[9], (D, BUNDLES * BUNDLE), D ** -0.5, 0.0625, ((1, 128),))
    up_weight = centred(key_list[10], (D, BUNDLES * BUNDLE), D ** -0.5, 0.0625, ((1, 128),))
    down_weight = centred(key_list[11], (BUNDLES * BUNDLE, D), (TOP * BUNDLE) ** -0.5, 0.125, ((0, 128),))
    return dict(queries=queries, new_keys=new_keys, token_values=token_values, key_cache=key_cache, stored_values=stored_values, cache_lengths=cache_lengths, residual=residual, norm_gain=norm_gain, active=active, gate_weight=gate_weight, up_weight=up_weight, down_weight=down_weight)


epsilon = 1e-05

def attend(queries, new_keys, token_values, key_cache, stored_values, cache_lengths):
    request_count, query_width = queries.shape
    kv_width = new_keys.shape[1]
    kv_heads = kv_width // HEAD_SIZE
    group_width = query_width // kv_width
    scaling = HEAD_SIZE ** (-0.5)
    grouped = queries.reshape(request_count, kv_heads, group_width, HEAD_SIZE).astype(jnp.float32)
    cached_keys = key_cache.reshape(request_count, CACHE_POSITIONS, kv_heads, HEAD_SIZE).astype(jnp.float32)
    cached_values = stored_values.reshape(request_count, CACHE_POSITIONS, kv_heads, HEAD_SIZE).astype(jnp.float32)
    scores = jnp.einsum('rkgd,rckd->rkgc', grouped, cached_keys) * scaling
    visible = jnp.arange(CACHE_POSITIONS, dtype=jnp.int32)[None, :] < cache_lengths[:, None]
    scores = jnp.where(visible[:, None, None, :], scores, -jnp.inf)
    fresh_keys = new_keys.reshape(request_count, kv_heads, HEAD_SIZE).astype(jnp.float32)
    fresh_score = jnp.einsum('rkgd,rkd->rkg', grouped, fresh_keys) * scaling
    highest = jnp.maximum(lax.optimization_barrier(jnp.max(scores, axis=-1)), fresh_score)
    weights_cache = jnp.exp(scores - highest[..., None])
    weight_fresh = jnp.exp(fresh_score - highest)
    denominator = lax.optimization_barrier(jnp.sum(weights_cache, axis=-1)) + weight_fresh
    probs_cache = (weights_cache / denominator[..., None]).astype(jnp.bfloat16)
    prob_fresh = (weight_fresh / denominator).astype(jnp.bfloat16)
    blended = jnp.einsum('rkgc,rckd->rkgd', probs_cache.astype(jnp.float32), cached_values)
    fresh_values = token_values.reshape(request_count, kv_heads, 1, HEAD_SIZE).astype(jnp.float32)
    blended = blended + prob_fresh[..., None].astype(jnp.float32) * fresh_values
    return blended.reshape(request_count, query_width).astype(jnp.bfloat16)

def reference(queries, new_keys, token_values, key_cache, stored_values, cache_lengths, residual, norm_gain, active, gate_weight, up_weight, down_weight):

    def attend_row(row_args):
        return attend(*[member[None] for member in row_args])[0]
    context = lax.map(attend_row, (queries, new_keys, token_values, key_cache, stored_values, cache_lengths))
    stream = residual.astype(jnp.float32) + context.astype(jnp.float32)
    mean_square = lax.optimization_barrier(jnp.mean(stream * stream, axis=1, keepdims=True))
    normed = (stream * lax.rsqrt(mean_square + epsilon) * norm_gain[None, :]).astype(jnp.bfloat16)
    offsets = jnp.arange(BUNDLE, dtype=jnp.int32)

    def feed_row(bundle_args):
        row_vector, chosen_bundles = bundle_args
        columns = (chosen_bundles[:, None].astype(jnp.int32) * BUNDLE + offsets[None, :]).reshape(-1)
        gate_value = jnp.dot(row_vector[None, :], jnp.take(gate_weight, columns, axis=1), preferred_element_type=jnp.float32)
        up_value = jnp.dot(row_vector[None, :], jnp.take(up_weight, columns, axis=1), preferred_element_type=jnp.float32)
        hidden = (jax.nn.relu(gate_value) * up_value).astype(jnp.bfloat16)
        return jnp.dot(hidden, jnp.take(down_weight, columns, axis=0), preferred_element_type=jnp.float32)[0]
    update = lax.map(feed_row, (normed, active))
    return (stream + update).astype(jnp.bfloat16)
```

```python
import jax
import jax.numpy as jnp
from jax import lax
from jax.sharding import PartitionSpec as P

HEAD_SIZE = 128
CACHE_POSITIONS = 256


epsilon = 1e-05


def attend(queries, new_keys, token_values, key_cache, stored_values, cache_lengths):
    request_count, query_width = queries.shape
    kv_width = new_keys.shape[1]
    kv_heads = kv_width // HEAD_SIZE
    group_width = query_width // kv_width
    scaling = HEAD_SIZE ** (-0.5)
    grouped = queries.reshape(request_count, kv_heads, group_width, HEAD_SIZE)
    cached_keys = key_cache.reshape(request_count, CACHE_POSITIONS, kv_heads, HEAD_SIZE)
    cached_values = stored_values.reshape(request_count, CACHE_POSITIONS, kv_heads, HEAD_SIZE)
    scores = (
        jnp.einsum("rkgd,rckd->rkgc", grouped, cached_keys, preferred_element_type=jnp.float32)
        * scaling
    )
    visible = jnp.arange(CACHE_POSITIONS, dtype=jnp.int32)[None, :] < cache_lengths[:, None]
    scores = jnp.where(visible[:, None, None, :], scores, -jnp.inf)
    fresh_keys = new_keys.reshape(request_count, kv_heads, HEAD_SIZE)
    fresh_score = (
        jnp.einsum("rkgd,rkd->rkg", grouped, fresh_keys, preferred_element_type=jnp.float32)
        * scaling
    )
    highest = jnp.maximum(jnp.max(scores, axis=-1), fresh_score)
    weights_cache = jnp.exp(scores - highest[..., None])
    weight_fresh = jnp.exp(fresh_score - highest)
    denominator = jnp.sum(weights_cache, axis=-1) + weight_fresh
    probs_cache = (weights_cache / denominator[..., None]).astype(jnp.bfloat16)
    prob_fresh = (weight_fresh / denominator).astype(jnp.bfloat16)
    blended = jnp.einsum(
        "rkgc,rckd->rkgd", probs_cache, cached_values, preferred_element_type=jnp.float32
    )
    fresh_values = token_values.reshape(request_count, kv_heads, 1, HEAD_SIZE).astype(jnp.float32)
    blended = blended + prob_fresh[..., None].astype(jnp.float32) * fresh_values
    return blended.reshape(request_count, query_width).astype(jnp.bfloat16)


def feed_forward(row_block, gate_weight, up_weight, selected):
    gate_value = jnp.dot(row_block, gate_weight, preferred_element_type=jnp.float32)
    up_value = jnp.dot(row_block, up_weight, preferred_element_type=jnp.float32)
    return (jax.nn.relu(gate_value) * up_value * selected).astype(jnp.bfloat16)


def shards(
    queries,
    new_keys,
    token_values,
    key_cache,
    stored_values,
    cache_lengths,
    residual,
    norm_gain,
    active,
    gate_weight,
    up_weight,
    down_weight,
):
    context = attend(queries, new_keys, token_values, key_cache, stored_values, cache_lengths)
    context = lax.all_to_all(context, "tp", split_axis=0, concat_axis=1, tiled=True)
    stream = residual.astype(jnp.float32) + context.astype(jnp.float32)
    mean_square = jnp.mean(stream * stream, axis=1, keepdims=True)
    normed = (stream * lax.rsqrt(mean_square + epsilon) * norm_gain[None, :]).astype(jnp.bfloat16)
    axes = ("sec", "dev", "tp")
    bundle = lax.axis_index(axes)
    named = jnp.any(active[:, :, None] == jnp.arange(128, dtype=jnp.int32)[None, None, :], axis=1)
    packed = jnp.concatenate([normed, named.astype(jnp.bfloat16)], axis=1)
    gathered = lax.all_gather(packed, axes, axis=0, tiled=True)
    rows = gathered[:, :8192]
    wanted = jnp.sum(
        jnp.where(jnp.arange(128)[None, :] == bundle, gathered[:, 8192:].astype(jnp.float32), 0.0),
        axis=1,
        keepdims=True,
    )
    hidden = feed_forward(rows, gate_weight, up_weight, wanted)
    terms = jnp.dot(hidden, down_weight, preferred_element_type=jnp.float32).astype(jnp.bfloat16)
    terms = terms.reshape(128, 32, 1024)
    update = lax.psum_scatter(terms, axes, scatter_dimension=0, tiled=False).reshape(4, 8192)
    return (stream + update.astype(jnp.float32)).astype(jnp.bfloat16)


def solution(mesh):
    return jax.shard_map(
        shards,
        mesh=mesh,
        in_specs=(
            P(("sec", "dev"), "tp"),
            P(("sec", "dev"), "tp"),
            P(("sec", "dev"), "tp"),
            P(("sec", "dev"), None, "tp"),
            P(("sec", "dev"), None, "tp"),
            P(("sec", "dev")),
            P(("sec", "dev", "tp"), None),
            P(),
            P(("sec", "dev", "tp"), None),
            P(None, ("sec", "dev", "tp")),
            P(None, ("sec", "dev", "tp")),
            P(("sec", "dev", "tp"), None),
        ),
        out_specs=P(("sec", "dev", "tp"), None),
        check_vma=False,
    )
```

```python
import functools

import jax
import jax.numpy as jnp
from jax import lax
from jax.experimental import pallas as pl
from jax.experimental.pallas import tpu as pltpu
from jax.sharding import PartitionSpec as P

MESH = pl.DeviceIdType.MESH
EPSILON = 1e-05
F32 = jnp.float32
BF16 = jnp.bfloat16

ROWS = 8
HALF = 4096
WIDTH = HALF + 128
SPANS = ((0, 1408), (1408, 2816), (2816, 4224))
TERMS = ((0, 1408), (1408, 2816), (2816, 4096))
ORDERS = (("x", "y", "z"), ("y", "z", "x"), ("z", "x", "y"))
COPIES = 256


def cut(lo, hi):
    middle = lo + ((hi - lo) // 128 + 1) // 2 * 128
    return (lo, middle), (middle, hi)


def kernel(
    lengths, queries, new_keys, token_values, residual, gain, active,
    key_cache, stored_values, gate, up, down,
    out,
    keys, values, w, d, g, acc, hid, stream, scores, probs, blend, other_resid, to_tp, from_tp,
    send_two, send_plus, send_minus, got_two_plus, got_two_minus, got_plus, got_minus, total,
    line_two, line_plus, line_minus, line_got_two_plus, line_got_two_minus, line_got_plus, line_got_minus,
    unit_two, unit_plus, unit_minus, unit_got_two, unit_got_plus, unit_got_minus,
    send_sems, recv_sems, local_sems,
):
    sec, dev, tp = lax.axis_index("sec"), lax.axis_index("dev"), lax.axis_index("tp")
    core = lax.rem(dev, 2)
    here = {"x": lax.rem(dev // 2, 4), "y": sec * 2 + tp, "z": dev // 8}

    def device(x, y, z, core):
        return (y // 2, (z * 4 + x) * 2 + core, lax.rem(y, 2))

    def along(dim, step):
        at = dict(here)
        at[dim] = lax.rem(here[dim] + step + 4, 4)
        return device(at["x"], at["y"], at["z"], core)

    twin = device(here["x"], here["y"], here["z"], 1 - core)
    pair = (sec, dev, 1 - tp)

    started = []

    def send(src, dst, target):
        i = len(started)
        copy = pltpu.make_async_remote_copy(
            src_ref=src, dst_ref=dst, send_sem=send_sems.at[i], recv_sem=recv_sems.at[i],
            device_id=target, device_id_type=MESH,
        )
        copy.start()
        started.append(copy)
        return i

    def arrive(i, dst):
        pltpu.make_async_remote_copy(
            src_ref=dst, dst_ref=dst, send_sem=send_sems.at[i], recv_sem=recv_sems.at[i],
            device_id=twin, device_id_type=MESH,
        ).wait_recv()

    local = []

    def fetch(src, dst):
        copy = pltpu.make_async_copy(src, dst, local_sems.at[len(local)])
        copy.start()
        local.append(copy)
        return copy

    key_rows = [fetch(key_cache.at[r], keys.at[r]) for r in range(ROWS)]
    value_rows = [fetch(stored_values.at[r], values.at[r]) for r in range(ROWS)]
    mine = pl.ds(pl.multiple_of(core * 128, 128), 128)
    mine_up = pl.ds(pl.multiple_of(256 + core * 128, 128), 128)
    pieces = []
    for t in range(2):
        rows = slice(t * HALF, (t + 1) * HALF)
        pieces.append((gate.at[rows, :], w.at[t, :, mine]))
        pieces.append((up.at[rows, :], w.at[t, :, mine_up]))
    for t in range(2):
        pieces.append((down.at[:, slice(t * HALF, (t + 1) * HALF)], d.at[t, mine, :]))
    weights = [fetch(src, dst) for src, dst in pieces]

    barrier = pltpu.get_barrier_semaphore()
    greeted = [twin] + [along(dim, step) for dim in ("x", "y", "z") for step in (1, -1)]
    for target in greeted:
        pl.semaphore_signal(barrier, inc=1, device_id=target, device_id_type=MESH)
    pl.semaphore_wait(barrier, len(greeted))

    theirs_half = pl.ds(pl.multiple_of((1 - tp) * HALF, 128), HALF)
    resid_id = send(residual.at[:, theirs_half], other_resid, pair)
    weight_ids = [send(src, dst, twin) for src, dst in pieces]

    first = tp == 0
    scale = 128 ** (-0.5)
    row_of = lax.rem(lax.broadcasted_iota(jnp.int32, (64, 1), 0), ROWS)
    limit = jnp.zeros((64, 1), jnp.int32)
    for r in range(ROWS):
        limit = jnp.where(row_of == r, lengths[r], limit)
    grouped = []
    for j in range(4):
        grouped.append(jnp.concatenate(
            [queries[:, (j * 8 + i) * 128:(j * 8 + i + 1) * 128].astype(F32) for i in range(8)], axis=0))
    for r in range(ROWS):
        key_rows[r].wait()
        for j in range(4):
            s = lax.dot_general(
                grouped[j].astype(BF16), keys[r, :, j * 128:(j + 1) * 128], (((1,), (1,)), ((), ())),
                preferred_element_type=F32)
            scores[j] = s if r == 0 else jnp.where(row_of == r, s, scores[j])
    column = lax.broadcasted_iota(jnp.int32, (64, 256), 1)
    fresh_probs = []
    for j in range(4):
        s = jnp.where(column < limit, scores[j] * scale, -1e30)
        fresh_key = jnp.concatenate([new_keys[:, j * 128:(j + 1) * 128].astype(F32)] * 8, axis=0)
        fresh = jnp.sum(grouped[j] * fresh_key, axis=1, keepdims=True) * scale
        highest = jnp.maximum(jnp.max(s, axis=1, keepdims=True), fresh)
        e = jnp.exp(s - highest)
        fresh_e = jnp.exp(fresh - highest)
        denominator = jnp.sum(e, axis=1, keepdims=True) + fresh_e
        probs[j] = (e / denominator).astype(BF16)
        fresh_probs.append((fresh_e / denominator).astype(BF16).astype(F32))
    for r in range(ROWS):
        value_rows[r].wait()
        for j in range(4):
            o = jnp.dot(probs[j], values[r, :, j * 128:(j + 1) * 128], preferred_element_type=F32)
            blend[j] = o if r == 0 else jnp.where(row_of == r, o, blend[j])

    lane = lax.broadcasted_iota(jnp.int32, (4, 128), 1)
    named = jnp.zeros((4, 128), F32)
    for k in range(16):
        named = jnp.where(active[:, k:k + 1] == lane, 1.0, named)

    arrive(resid_id, other_resid)
    me = (here["y"], here["z"], here["x"])
    squares = jnp.zeros((ROWS, 128), F32)
    for j in range(4):
        fresh_value = jnp.concatenate([token_values[:, j * 128:(j + 1) * 128].astype(F32)] * 8, axis=0)
        block = (blend[j] + fresh_probs[j] * fresh_value).astype(BF16).astype(F32)
        for i in range(8):
            lo = (j * 8 + i) * 128
            own = jnp.where(first, residual[:, lo:lo + 128], residual[:, HALF + lo:HALF + lo + 128]).astype(F32)
            other = other_resid[:, lo:lo + 128].astype(F32)
            resid = jnp.concatenate(
                [jnp.where(first, own, other), jnp.where(first, other, own)], axis=0)
            value = resid + block[i * 8:(i + 1) * 8]
            stream[:, lo:lo + 128] = value
            squares = squares + value * value
            factor = jnp.where(first, gain[:, lo:lo + 128], gain[:, HALF + lo:HALF + lo + 128])
            g[me + (slice(None), slice(lo, lo + 128))] = (value * factor).astype(BF16)
    sub8 = lax.broadcasted_iota(jnp.int32, (ROWS, 128), 0)
    lane8 = lax.broadcasted_iota(jnp.int32, (ROWS, 128), 1)
    row_sums = jnp.sum(squares, axis=1, keepdims=True)
    sums = jnp.sum(jnp.where(sub8 == lane8, row_sums, 0.0), axis=0, keepdims=True)
    sums_hi = sums.astype(BF16).astype(F32)
    sums_lo = sums - sums_hi
    lower = lax.broadcasted_iota(jnp.int32, (4, 128), 0)
    told = jnp.where(lower == 0, sums_hi, jnp.where(lower == 1, sums_lo, 0.0))
    extra = jnp.concatenate([jnp.where(first, named, told), jnp.where(first, told, named)], axis=0)
    g[me + (slice(None), slice(HALF, WIDTH))] = extra.astype(BF16)

    def spot(at, columns):
        index = tuple(at[dim] if dim in at else slice(None) for dim in ("y", "z", "x"))
        return g.at[index + (slice(None), slice(*columns))]

    def near(dim, step):
        return lax.rem(here[dim] + step + 4, 4)

    class Ring:
        def __init__(self, k, dim, fixed):
            self.columns, self.dim, self.fixed = SPANS[k], dim, fixed

        def region(self, step, columns):
            at = dict(self.fixed)
            at[self.dim] = near(self.dim, step)
            return spot(at, columns)

        def open(self):
            part = self.region(0, self.columns)
            self.plus = send(part, part, along(self.dim, 1))
            self.minus = send(part, part, along(self.dim, -1))

        def relay(self):
            one, two = cut(*self.columns)
            arrive(self.plus, self.region(-1, self.columns))
            part = self.region(-1, one)
            self.far_one = send(part, part, along(self.dim, 1))
            arrive(self.minus, self.region(1, self.columns))
            part = self.region(1, two)
            self.far_two = send(part, part, along(self.dim, -1))

        def close(self):
            one, two = cut(*self.columns)
            arrive(self.far_one, self.region(2, one))
            arrive(self.far_two, self.region(2, two))

    parts = range(3)
    rings = []
    for k in parts:
        a, b, c = ORDERS[k]
        units = Ring(k, a, {b: here[b], c: here[c]})
        lines = Ring(k, b, {c: here[c]})
        slabs = {step: Ring(k, c, {b: near(b, step)}) for step in (0, -1, 1, 2)}
        rings.append((units, lines, slabs))

    def multiply(k, step):
        lo, hi = SPANS[k][0], min(SPANS[k][1], HALF)
        c = ORDERS[k][2]
        at = near(c, step)
        columns = slice(lo, hi)
        n = hi - lo
        if c == "y":
            rows = g[at, :, :, :, columns].reshape(128, n)
            part = jnp.dot(rows, w[lax.rem(at, 2), columns, :], preferred_element_type=F32)
            acc[at // 2] += part.reshape(4, 4, ROWS, 512)
            return
        part = 0.0
        for t in range(2):
            if c == "z":
                rows = jnp.concatenate([g[y, at, :, :, columns].reshape(32, n) for y in (t, 2 + t)], axis=0)
            else:
                rows = jnp.concatenate([g[y, :, at, :, columns].reshape(32, n) for y in (t, 2 + t)], axis=0)
            part = part + jnp.dot(rows, w[t, columns, :], preferred_element_type=F32)
        part = part.reshape(2, 4, ROWS, 512)
        if c == "z":
            acc[:, at] += part
        else:
            acc[:, :, at] += part

    for k in parts:
        rings[k][0].open()
    acc[...] = jnp.zeros_like(acc)
    for k in parts:
        rings[k][0].relay()
    for k in parts:
        rings[k][0].close()
        rings[k][1].open()
        rings[k][2][0].open()
    for k in parts:
        rings[k][1].relay()
        rings[k][2][-1].open()
        rings[k][2][1].open()
    for k in parts:
        rings[k][2][0].relay()
    for k in parts:
        rings[k][1].close()
        rings[k][2][2].open()
    for copy in weights[:4]:
        copy.wait()
    for i in range(4):
        arrive(weight_ids[i], w.at[i // 2, :, pl.ds(pl.multiple_of((1 - core) * 128 + i % 2 * 256, 128), 128)])
    for k in parts:
        multiply(k, 0)
    for step in (-1, 1, 2):
        for k in parts:
            rings[k][2][step].relay()
    for k in parts:
        multiply(k, -1)
        multiply(k, 1)
    for k in parts:
        for step in (0, -1, 1, 2):
            rings[k][2][step].close()
        multiply(k, 2)

    sub = lax.broadcasted_iota(jnp.int32, (32, ROWS, 128), 1)
    lanes = lax.broadcasted_iota(jnp.int32, (32, ROWS, 128), 2)
    extras = []
    for t in range(2):
        extras.append(jnp.concatenate(
            [g[y, :, :, :, HALF:WIDTH].astype(F32).reshape(16, ROWS, 128) for y in (t, 2 + t)], axis=0))
    names = jnp.where(sub < 4, extras[0], extras[1])
    bundle = sec * 64 + (dev - core) * 2 + tp
    wanted = [
        jnp.sum(jnp.where(lanes == bundle + 2 * i, names, 0.0), axis=2, keepdims=True).reshape(256, 1)
        for i in range(2)
    ]
    sums = (extras[0][:, 4:5] + extras[0][:, 5:6]) + (extras[1][:, 0:1] + extras[1][:, 1:2])
    mean = jnp.sum(jnp.where(lanes == sub, sums, 0.0), axis=2, keepdims=True).reshape(256, 1) / 8192.0
    inverse = lax.rsqrt(mean + EPSILON)
    gate_value = acc[:, :, :, :, 0:256].reshape(256, 256) * inverse
    up_value = acc[:, :, :, :, 256:512].reshape(256, 256) * inverse
    low = lax.broadcasted_iota(jnp.int32, (256, 256), 1) < 128
    hidden = jnp.maximum(gate_value, 0.0) * up_value * jnp.where(low, wanted[0], wanted[1])
    hid[...] = hidden.astype(BF16).reshape(2, 4, 4, ROWS, 256)

    for copy in weights[4:]:
        copy.wait()
    for i in range(2):
        arrive(weight_ids[4 + i], d.at[i, pl.ds(pl.multiple_of((1 - core) * 128, 128), 128), :])

    def terms(k, step, store):
        c = ORDERS[k][2]
        at = near(c, step)
        columns = slice(*TERMS[k])
        n = TERMS[k][1] - TERMS[k][0]
        if c == "y":
            rows = hid[at // 2].reshape(128, 256)
            part = jnp.dot(rows, d[lax.rem(at, 2), :, columns], preferred_element_type=F32)
            store(slice(None), part.reshape(4, 4, ROWS, n))
            return
        rows = (hid[:, at] if c == "z" else hid[:, :, at]).reshape(64, 256)
        for t in range(2):
            part = jnp.dot(rows, d[t, :, columns], preferred_element_type=F32).reshape(2, 4, ROWS, n)
            store(t, part[0])
            store(2 + t, part[1])

    def width(k):
        return TERMS[k][1] - TERMS[k][0]

    def line(ref, k, step, columns=None):
        a, b, c = ORDERS[k]
        at = near(b, step)
        columns = slice(0, width(k)) if columns is None else slice(*columns)
        lead = (at,) if b == "y" else (slice(None), at)
        rest = (slice(None),) if b == "y" else ()
        return ref.at[(k,) + lead + rest + (slice(None), columns)]

    def fill(ref, k):
        def store(y, value):
            if isinstance(y, slice):
                ref[k, :, :, :, 0:width(k)] = value.astype(ref.dtype)
            else:
                ref[k, y, :, :, 0:width(k)] = value.astype(ref.dtype)
        return store

    order = (2, 1, -1, 0)
    ids = {}
    for k in parts:
        c = ORDERS[k][2]
        one, two = cut(0, width(k))
        terms(k, 2, fill(send_two, k))
        for step in order:
            ids[k, step, "two_plus"] = send(line(send_two, k, step, one), line(got_two_plus, k, step, one), along(c, 1))
            ids[k, step, "two_minus"] = send(line(send_two, k, step, two), line(got_two_minus, k, step, two), along(c, -1))
    for k in parts:
        c = ORDERS[k][2]
        one, two = cut(0, width(k))
        terms(k, 1, fill(send_plus, k))
        terms(k, -1, fill(send_minus, k))
        for step in order:
            ids[k, step, "plus_two"] = send(line(send_plus, k, step, two), line(got_plus, k, step, two), along(c, 1))
            ids[k, step, "minus_one"] = send(line(send_minus, k, step, one), line(got_minus, k, step, one), along(c, -1))
    for k in parts:
        terms(k, 0, fill(total, k))

    def add_into(ref, *others):
        value = ref[...].astype(F32)
        for other in others:
            value = value + other[...].astype(F32)
        ref[...] = value.astype(ref.dtype)

    for step in order:
        for k in parts:
            c = ORDERS[k][2]
            one, two = cut(0, width(k))
            arrive(ids[k, step, "two_plus"], line(got_two_plus, k, step, one))
            add_into(line(send_plus, k, step, one), line(got_two_plus, k, step, one))
            ids[k, step, "plus_one"] = send(line(send_plus, k, step, one), line(got_plus, k, step, one), along(c, 1))
            arrive(ids[k, step, "two_minus"], line(got_two_minus, k, step, two))
            add_into(line(send_minus, k, step, two), line(got_two_minus, k, step, two))
            ids[k, step, "minus_two"] = send(line(send_minus, k, step, two), line(got_minus, k, step, two), along(c, -1))

    for step in order:
        for k in parts:
            b = ORDERS[k][1]
            n = width(k)
            one, two = cut(0, n)
            one_s, two_s, all_s = slice(*one), slice(*two), slice(0, n)
            arrive(ids[k, step, "plus_two"], line(got_plus, k, step, two))
            arrive(ids[k, step, "plus_one"], line(got_plus, k, step, one))
            arrive(ids[k, step, "minus_one"], line(got_minus, k, step, one))
            arrive(ids[k, step, "minus_two"], line(got_minus, k, step, two))
            value = (line(total, k, step)[...] + line(got_plus, k, step)[...].astype(F32)
                     + line(got_minus, k, step)[...].astype(F32))
            if step == 2:
                line_two[k, :, :, all_s] = value.astype(BF16)
                ids[k, "two_plus"] = send(
                    line_two.at[k, :, :, one_s], line_got_two_plus.at[k, :, :, one_s], along(b, 1))
                ids[k, "two_minus"] = send(
                    line_two.at[k, :, :, two_s], line_got_two_minus.at[k, :, :, two_s], along(b, -1))
            elif step == 1:
                line_plus[k, :, :, all_s] = value.astype(BF16)
                ids[k, "plus_two"] = send(
                    line_plus.at[k, :, :, two_s], line_got_plus.at[k, :, :, two_s], along(b, 1))
            elif step == -1:
                line_minus[k, :, :, all_s] = value.astype(BF16)
                ids[k, "minus_one"] = send(
                    line_minus.at[k, :, :, one_s], line_got_minus.at[k, :, :, one_s], along(b, -1))
            else:
                line(total, k, 0)[...] = value
            if step == -1:
                arrive(ids[k, "two_plus"], line_got_two_plus.at[k, :, :, one_s])
                add_into(line_plus.at[k, :, :, one_s], line_got_two_plus.at[k, :, :, one_s])
                ids[k, "plus_one"] = send(
                    line_plus.at[k, :, :, one_s], line_got_plus.at[k, :, :, one_s], along(b, 1))
                arrive(ids[k, "two_minus"], line_got_two_minus.at[k, :, :, two_s])
                add_into(line_minus.at[k, :, :, two_s], line_got_two_minus.at[k, :, :, two_s])
                ids[k, "minus_two"] = send(
                    line_minus.at[k, :, :, two_s], line_got_minus.at[k, :, :, two_s], along(b, -1))

    for k in parts:
        a = ORDERS[k][0]
        n = width(k)
        one, two = cut(0, n)
        one_s, two_s, all_s = slice(*one), slice(*two), slice(0, n)
        arrive(ids[k, "plus_two"], line_got_plus.at[k, :, :, two_s])
        arrive(ids[k, "plus_one"], line_got_plus.at[k, :, :, one_s])
        arrive(ids[k, "minus_one"], line_got_minus.at[k, :, :, one_s])
        arrive(ids[k, "minus_two"], line_got_minus.at[k, :, :, two_s])
        add_into(line(total, k, 0), line_got_plus.at[k, :, :, all_s], line_got_minus.at[k, :, :, all_s])
        whole = line(total, k, 0)
        unit_two[k, :, all_s] = whole.at[near(a, 2)][...].astype(BF16)
        ids[k, "unit_two"] = send(unit_two.at[k, :, all_s], unit_got_two.at[k, :, all_s], along(a, 1))
        unit_minus[k, :, all_s] = whole.at[near(a, -1)][...].astype(BF16)
        ids[k, "unit_minus"] = send(unit_minus.at[k, :, all_s], unit_got_minus.at[k, :, all_s], along(a, -1))
    for k in parts:
        a = ORDERS[k][0]
        all_s = slice(0, width(k))
        arrive(ids[k, "unit_two"], unit_got_two.at[k, :, all_s])
        value = line(total, k, 0).at[near(a, 1)][...] + unit_got_two[k, :, all_s].astype(F32)
        unit_plus[k, :, all_s] = value.astype(BF16)
        ids[k, "unit_plus"] = send(unit_plus.at[k, :, all_s], unit_got_plus.at[k, :, all_s], along(a, 1))
    kept = []
    for k in parts:
        a = ORDERS[k][0]
        all_s = slice(0, width(k))
        arrive(ids[k, "unit_minus"], unit_got_minus.at[k, :, all_s])
        arrive(ids[k, "unit_plus"], unit_got_plus.at[k, :, all_s])
        value = (line(total, k, 0).at[near(a, 0)][...] + unit_got_plus[k, :, all_s].astype(F32)
                 + unit_got_minus[k, :, all_s].astype(F32))
        value = stream[:, slice(*TERMS[k])] + value
        kept.append(jnp.where(first, value[0:4], value[4:8]).astype(BF16))
        to_tp[:, slice(*TERMS[k])] = jnp.where(first, value[4:8], value[0:4]).astype(BF16)
    last = send(to_tp, from_tp, pair)
    arrive(last, from_tp)
    for k in parts:
        lo, hi = TERMS[k]
        theirs = from_tp[:, lo:hi]
        out[:, lo:hi] = jnp.where(first, kept[k], theirs)
        out[:, HALF + lo:HALF + hi] = jnp.where(first, theirs, kept[k])
    for copy in started:
        copy.wait_send()


def shards(
    queries, new_keys, token_values, key_cache, stored_values, cache_lengths, residual, norm_gain,
    active, gate_weight, up_weight, down_weight,
):
    vmem = pl.BlockSpec(memory_space=pltpu.VMEM)
    hbm = pl.BlockSpec(memory_space=pl.ANY)
    slab = (3, 4, 4, ROWS, 1408)
    rows = (3, 4, ROWS, 1408)
    unit = (3, ROWS, 1408)
    return pl.pallas_call(
        kernel,
        out_shape=jax.ShapeDtypeStruct((4, 8192), BF16),
        in_specs=[pl.BlockSpec(memory_space=pltpu.SMEM)] + [vmem] * 6 + [hbm] * 5,
        out_specs=vmem,
        scratch_shapes=[
            pltpu.VMEM((ROWS, 256, 512), BF16),
            pltpu.VMEM((ROWS, 256, 512), BF16),
            pltpu.VMEM((2, HALF, 512), BF16),
            pltpu.VMEM((2, 256, HALF), BF16),
            pltpu.VMEM((4, 4, 4, ROWS, WIDTH), BF16),
            pltpu.VMEM((2, 4, 4, ROWS, 512), F32),
            pltpu.VMEM((2, 4, 4, ROWS, 256), BF16),
            pltpu.VMEM((ROWS, HALF), F32),
            pltpu.VMEM((4, 64, 256), F32),
            pltpu.VMEM((4, 64, 256), BF16),
            pltpu.VMEM((4, 64, 128), F32),
            pltpu.VMEM((4, HALF), BF16),
            pltpu.VMEM((4, HALF), BF16),
            pltpu.VMEM((4, HALF), BF16),
        ]
        + [pltpu.VMEM(slab, BF16)] * 7
        + [pltpu.VMEM(slab, F32)]
        + [pltpu.VMEM(rows, BF16)] * 7
        + [pltpu.VMEM(unit, BF16)] * 6
        + [
            pltpu.SemaphoreType.DMA((COPIES,)),
            pltpu.SemaphoreType.DMA((COPIES,)),
            pltpu.SemaphoreType.DMA((32,)),
        ],
        compiler_params=pltpu.CompilerParams(
            collective_id=0, has_side_effects=True, vmem_limit_bytes=60 * 2**20),
    )(cache_lengths, queries, new_keys, token_values, residual, norm_gain.reshape(1, 8192), active,
      key_cache, stored_values, gate_weight, up_weight, down_weight)


def solution(mesh):
    return jax.shard_map(
        shards,
        mesh=mesh,
        in_specs=(
            P(("sec", "dev"), "tp"),
            P(("sec", "dev"), "tp"),
            P(("sec", "dev"), "tp"),
            P(("sec", "dev"), None, "tp"),
            P(("sec", "dev"), None, "tp"),
            P(("sec", "dev")),
            P(("sec", "dev", "tp"), None),
            P(),
            P(("sec", "dev", "tp"), None),
            P(None, ("sec", "dev", "tp")),
            P(None, ("sec", "dev", "tp")),
            P(("sec", "dev", "tp"), None),
        ),
        out_specs=P(("sec", "dev", "tp"), None),
        check_vma=False,
    )
```

```python
import functools

import jax
import jax.numpy as jnp
from jax import lax
from jax.experimental import pallas as pl
from jax.experimental.pallas import tpu as pltpu
from jax.sharding import PartitionSpec as P

MESH = pl.DeviceIdType.MESH
EPSILON = 1e-05
F32 = jnp.float32
BF16 = jnp.bfloat16

ROWS = 8
HALF = 4096
WIDTH = HALF + 128
SPANS = ((0, 1408), (1408, 2816), (2816, 4224))
TERMS = ((0, 1408), (1408, 2816), (2816, 4096))
ORDERS = (("x", "y", "z"), ("y", "z", "x"), ("z", "x", "y"))
SENDS = 10
ARRIVALS = 128
FETCHES = 18


def cut(lo, hi):
    middle = lo + ((hi - lo) // 128 + 1) // 2 * 128
    return (lo, middle), (middle, hi)


def kernel(
    lengths, queries, new_keys, token_values, residual, gain, active,
    key_cache, stored_values, gate, up, down,
    out,
    keys, values, w, d, g, acc, hid, stream, scores, probs, blend, other_resid, to_tp, from_tp,
    send_two, send_plus, send_minus, got_two_plus, got_two_minus, got_plus, got_minus, total,
    line_two, line_plus, line_minus, line_got_two_plus, line_got_two_minus, line_got_plus, line_got_minus,
    unit_two, unit_plus, unit_minus, unit_got_two, unit_got_plus, unit_got_minus,
    send_sems, recv_sems, local_sems,
):
    sec, dev, tp = lax.axis_index("sec"), lax.axis_index("dev"), lax.axis_index("tp")
    core = lax.rem(dev, 2)
    here = {"x": lax.rem(dev // 2, 4), "y": sec * 2 + tp, "z": dev // 8}

    def device(x, y, z, core):
        return (y // 2, (z * 4 + x) * 2 + core, lax.rem(y, 2))

    def along(dim, step):
        at = dict(here)
        at[dim] = lax.rem(here[dim] + step + 4, 4)
        return device(at["x"], at["y"], at["z"], core)

    twin = device(here["x"], here["y"], here["z"], 1 - core)
    pair = (sec, dev, 1 - tp)

    used = []

    def arrival():
        used.append(None)
        return len(used) - 1

    def send(group, i, src, dst, target):
        pltpu.make_async_remote_copy(
            src_ref=src, dst_ref=dst, send_sem=send_sems.at[group], recv_sem=recv_sems.at[i],
            device_id=target, device_id_type=MESH,
        ).start()

    def arrive(i, dst):
        pltpu.make_async_remote_copy(
            src_ref=dst, dst_ref=dst, send_sem=send_sems.at[0], recv_sem=recv_sems.at[i],
            device_id=twin, device_id_type=MESH,
        ).wait_recv()

    def sent(group, src):
        pltpu.make_async_remote_copy(
            src_ref=src, dst_ref=src, send_sem=send_sems.at[group], recv_sem=recv_sems.at[0],
            device_id=twin, device_id_type=MESH,
        ).wait_send()

    def fetch(src, dst, i):
        copy = pltpu.make_async_copy(src, dst, local_sems.at[i])
        copy.start()
        return copy

    key_rows = [fetch(key_cache.at[r], keys.at[r], r) for r in range(ROWS)]
    value_rows = [fetch(stored_values.at[r], values.at[r], ROWS + r) for r in range(ROWS)]
    mine = pl.ds(pl.multiple_of(core * 128, 128), 128)
    mine_up = pl.ds(pl.multiple_of(256 + core * 128, 128), 128)
    pieces = []
    for t in range(2):
        rows = slice(t * HALF, (t + 1) * HALF)
        pieces.append((gate.at[rows, :], w.at[t, :, mine]))
        pieces.append((up.at[rows, :], w.at[t, :, mine_up]))
    for t in range(2):
        pieces.append((down.at[:, slice(t * HALF, (t + 1) * HALF)], d.at[t, mine, :]))
    for n, (src, dst) in enumerate(pieces):
        fetch(src, dst, 16 + n // 4)
    w_bytes, d_bytes = w.at[:, :, 0:256], d.at[:, 0:128, :]

    barrier = pltpu.get_barrier_semaphore()
    greeted = [twin] + [along(dim, step) for dim in ("x", "y", "z") for step in (1, -1)]
    for target in greeted:
        pl.semaphore_signal(barrier, inc=1, device_id=target, device_id_type=MESH)
    pl.semaphore_wait(barrier, len(greeted))

    theirs_half = pl.ds(pl.multiple_of((1 - tp) * HALF, 128), HALF)
    resid_id, w_id, d_id = arrival(), arrival(), arrival()
    send(0, resid_id, residual.at[:, theirs_half], other_resid, pair)
    for n, (src, dst) in enumerate(pieces):
        send(1 + n // 4, (w_id, d_id)[n // 4], src, dst, twin)

    first = tp == 0
    scale = 128 ** (-0.5)
    row_of = lax.rem(lax.broadcasted_iota(jnp.int32, (64, 1), 0), ROWS)
    limit = jnp.zeros((64, 1), jnp.int32)
    for r in range(ROWS):
        limit = jnp.where(row_of == r, lengths[r], limit)
    grouped = []
    for j in range(4):
        grouped.append(jnp.concatenate(
            [queries[:, (j * 8 + i) * 128:(j * 8 + i + 1) * 128].astype(F32) for i in range(8)], axis=0))
    for r in range(ROWS):
        key_rows[r].wait()
        for j in range(4):
            s = lax.dot_general(
                grouped[j].astype(BF16), keys[r, :, j * 128:(j + 1) * 128], (((1,), (1,)), ((), ())),
                preferred_element_type=F32)
            scores[j] = s if r == 0 else jnp.where(row_of == r, s, scores[j])
    column = lax.broadcasted_iota(jnp.int32, (64, 256), 1)
    fresh_probs = []
    for j in range(4):
        s = jnp.where(column < limit, scores[j] * scale, -1e30)
        fresh_key = jnp.concatenate([new_keys[:, j * 128:(j + 1) * 128].astype(F32)] * 8, axis=0)
        fresh = jnp.sum(grouped[j] * fresh_key, axis=1, keepdims=True) * scale
        highest = jnp.maximum(jnp.max(s, axis=1, keepdims=True), fresh)
        e = jnp.exp(s - highest)
        fresh_e = jnp.exp(fresh - highest)
        denominator = jnp.sum(e, axis=1, keepdims=True) + fresh_e
        probs[j] = (e / denominator).astype(BF16)
        fresh_probs.append((fresh_e / denominator).astype(BF16).astype(F32))
    for r in range(ROWS):
        value_rows[r].wait()
        for j in range(4):
            o = jnp.dot(probs[j], values[r, :, j * 128:(j + 1) * 128], preferred_element_type=F32)
            blend[j] = o if r == 0 else jnp.where(row_of == r, o, blend[j])

    lane = lax.broadcasted_iota(jnp.int32, (4, 128), 1)
    named = jnp.zeros((4, 128), F32)
    for k in range(16):
        named = jnp.where(active[:, k:k + 1] == lane, 1.0, named)

    arrive(resid_id, other_resid)
    me = (here["y"], here["z"], here["x"])
    squares = jnp.zeros((ROWS, 128), F32)
    for j in range(4):
        fresh_value = jnp.concatenate([token_values[:, j * 128:(j + 1) * 128].astype(F32)] * 8, axis=0)
        block = (blend[j] + fresh_probs[j] * fresh_value).astype(BF16).astype(F32)
        for i in range(8):
            lo = (j * 8 + i) * 128
            own = jnp.where(first, residual[:, lo:lo + 128], residual[:, HALF + lo:HALF + lo + 128]).astype(F32)
            other = other_resid[:, lo:lo + 128].astype(F32)
            resid = jnp.concatenate(
                [jnp.where(first, own, other), jnp.where(first, other, own)], axis=0)
            value = resid + block[i * 8:(i + 1) * 8]
            stream[:, lo:lo + 128] = value
            squares = squares + value * value
            factor = jnp.where(first, gain[:, lo:lo + 128], gain[:, HALF + lo:HALF + lo + 128])
            g[me + (slice(None), slice(lo, lo + 128))] = (value * factor).astype(BF16)
    sub8 = lax.broadcasted_iota(jnp.int32, (ROWS, 128), 0)
    lane8 = lax.broadcasted_iota(jnp.int32, (ROWS, 128), 1)
    row_sums = jnp.sum(squares, axis=1, keepdims=True)
    sums = jnp.sum(jnp.where(sub8 == lane8, row_sums, 0.0), axis=0, keepdims=True)
    sums_hi = sums.astype(BF16).astype(F32)
    sums_lo = sums - sums_hi
    lower = lax.broadcasted_iota(jnp.int32, (4, 128), 0)
    told = jnp.where(lower == 0, sums_hi, jnp.where(lower == 1, sums_lo, 0.0))
    extra = jnp.concatenate([jnp.where(first, named, told), jnp.where(first, told, named)], axis=0)
    g[me + (slice(None), slice(HALF, WIDTH))] = extra.astype(BF16)

    def spot(at, columns):
        index = tuple(at[dim] if dim in at else slice(None) for dim in ("y", "z", "x"))
        return g.at[index + (slice(None), slice(*columns))]

    def near(dim, step):
        return lax.rem(here[dim] + step + 4, 4)

    class Ring:
        def __init__(self, k, group, dim, fixed, far):
            self.columns, self.group, self.dim, self.fixed, self.far = SPANS[k], group, dim, fixed, far

        def region(self, step, columns):
            at = dict(self.fixed)
            at[self.dim] = near(self.dim, step)
            return spot(at, columns)

        def open(self):
            part = self.region(0, self.columns)
            self.plus, self.minus = arrival(), arrival()
            send(self.group, self.plus, part, part, along(self.dim, 1))
            send(self.group, self.minus, part, part, along(self.dim, -1))

        def relay(self):
            one, two = cut(*self.columns)
            arrive(self.plus, self.region(-1, self.columns))
            part = self.region(-1, one)
            send(self.group, self.far, part, part, along(self.dim, 1))
            arrive(self.minus, self.region(1, self.columns))
            part = self.region(1, two)
            send(self.group, self.far, part, part, along(self.dim, -1))

    parts = range(3)
    around = (0, 1, -1, 2)
    rings = []
    for k in parts:
        a, b, c = ORDERS[k]
        far = [arrival() for _ in range(3)]
        units = Ring(k, 3, a, {b: here[b], c: here[c]}, far[0])
        second = {step: Ring(k, 4, b, {a: near(a, step), c: here[c]}, far[1]) for step in around}
        third = {step: Ring(k, 5, c, {a: near(a, step), b: here[b]}, far[2]) for step in around}
        lines = {step: Ring(k, 5, c, {b: near(b, step)}, far[2]) for step in (1, -1, 2)}
        rings.append((units, second, third, lines))

    def close(k, phase):
        dims = ORDERS[k][:phase + 1]
        at = {dim: here[dim] for dim in ORDERS[k][phase + 1:]}
        at[dims[-1]] = near(dims[-1], 2)
        arrive(rings[k][phase].far if phase == 0 else rings[k][phase][0].far, spot(at, SPANS[k]))

    def multiply(k, step):
        lo, hi = SPANS[k][0], min(SPANS[k][1], HALF)
        c = ORDERS[k][2]
        at = near(c, step)
        columns = slice(lo, hi)
        n = hi - lo
        if c == "y":
            rows = g[at, :, :, :, columns].reshape(128, n)
            part = jnp.dot(rows, w[lax.rem(at, 2), columns, :], preferred_element_type=F32)
            acc[at // 2] += part.reshape(4, 4, ROWS, 512)
            return
        part = 0.0
        for t in range(2):
            if c == "z":
                rows = jnp.concatenate([g[y, at, :, :, columns].reshape(32, n) for y in (t, 2 + t)], axis=0)
            else:
                rows = jnp.concatenate([g[y, :, at, :, columns].reshape(32, n) for y in (t, 2 + t)], axis=0)
            part = part + jnp.dot(rows, w[t, columns, :], preferred_element_type=F32)
        part = part.reshape(2, 4, ROWS, 512)
        if c == "z":
            acc[:, at] += part
        else:
            acc[:, :, at] += part

    for phase in range(3):
        for k in parts:
            (rings[k][0] if phase == 0 else rings[k][phase][0]).open()
    acc[...] = jnp.zeros_like(acc)
    for k in parts:
        rings[k][0].relay()
    for phase in (1, 2):
        for k in parts:
            rings[k][phase][1].open()
            rings[k][phase][-1].open()
    for k in parts:
        rings[k][1][0].relay()
    for k in parts:
        close(k, 0)
        rings[k][1][2].open()
    for k in parts:
        rings[k][2][2].open()
    for k in parts:
        rings[k][2][0].relay()
    for k in parts:
        rings[k][1][1].relay()
        rings[k][1][-1].relay()
    for k in parts:
        rings[k][1][2].relay()
    for k in parts:
        rings[k][3][1].open()
        rings[k][3][-1].open()
    for k in parts:
        rings[k][2][1].relay()
        rings[k][2][-1].relay()
    for k in parts:
        close(k, 1)
        rings[k][3][2].open()
    pltpu.make_async_copy(w_bytes, w_bytes, local_sems.at[16]).wait()
    arrive(w_id, w_bytes)
    for k in parts:
        multiply(k, 0)
        rings[k][2][2].relay()
    for step in (1, -1, 2):
        for k in parts:
            rings[k][3][step].relay()
    for k in parts:
        multiply(k, -1)
        multiply(k, 1)
    for k in parts:
        close(k, 2)
        multiply(k, 2)

    sub = lax.broadcasted_iota(jnp.int32, (32, ROWS, 128), 1)
    lanes = lax.broadcasted_iota(jnp.int32, (32, ROWS, 128), 2)
    extras = []
    for t in range(2):
        extras.append(jnp.concatenate(
            [g[y, :, :, :, HALF:WIDTH].astype(F32).reshape(16, ROWS, 128) for y in (t, 2 + t)], axis=0))
    names = jnp.where(sub < 4, extras[0], extras[1])
    bundle = sec * 64 + (dev - core) * 2 + tp
    wanted = [
        jnp.sum(jnp.where(lanes == bundle + 2 * i, names, 0.0), axis=2, keepdims=True).reshape(256, 1)
        for i in range(2)
    ]
    sums = (extras[0][:, 4:5] + extras[0][:, 5:6]) + (extras[1][:, 0:1] + extras[1][:, 1:2])
    mean = jnp.sum(jnp.where(lanes == sub, sums, 0.0), axis=2, keepdims=True).reshape(256, 1) / 8192.0
    inverse = lax.rsqrt(mean + EPSILON)
    gate_value = acc[:, :, :, :, 0:256].reshape(256, 256) * inverse
    up_value = acc[:, :, :, :, 256:512].reshape(256, 256) * inverse
    low = lax.broadcasted_iota(jnp.int32, (256, 256), 1) < 128
    hidden = jnp.maximum(gate_value, 0.0) * up_value * jnp.where(low, wanted[0], wanted[1])
    hid[...] = hidden.astype(BF16).reshape(2, 4, 4, ROWS, 256)

    pltpu.make_async_copy(d_bytes, d_bytes, local_sems.at[17]).wait()
    arrive(d_id, d_bytes)

    def terms(k, step, store):
        c = ORDERS[k][2]
        at = near(c, step)
        columns = slice(*TERMS[k])
        n = TERMS[k][1] - TERMS[k][0]
        if c == "y":
            rows = hid[at // 2].reshape(128, 256)
            part = jnp.dot(rows, d[lax.rem(at, 2), :, columns], preferred_element_type=F32)
            store(slice(None), part.reshape(4, 4, ROWS, n))
            return
        rows = (hid[:, at] if c == "z" else hid[:, :, at]).reshape(64, 256)
        for t in range(2):
            part = jnp.dot(rows, d[t, :, columns], preferred_element_type=F32).reshape(2, 4, ROWS, n)
            store(t, part[0])
            store(2 + t, part[1])

    def width(k):
        return TERMS[k][1] - TERMS[k][0]

    def line(ref, k, step, columns=None):
        a, b, c = ORDERS[k]
        at = near(b, step)
        columns = slice(0, width(k)) if columns is None else slice(*columns)
        lead = (at,) if b == "y" else (slice(None), at)
        rest = (slice(None),) if b == "y" else ()
        return ref.at[(k,) + lead + rest + (slice(None), columns)]

    def fill(ref, k):
        def store(y, value):
            if isinstance(y, slice):
                ref[k, :, :, :, 0:width(k)] = value.astype(ref.dtype)
            else:
                ref[k, y, :, :, 0:width(k)] = value.astype(ref.dtype)
        return store

    def add_into(ref, *others):
        value = ref[...].astype(F32)
        for other in others:
            value = value + other[...].astype(F32)
        ref[...] = value.astype(ref.dtype)

    def halves(k):
        one, two = cut(0, width(k))
        return slice(*one), slice(*two), slice(0, width(k))

    ids = {(k, step, kind): arrival() for k in parts for step in around for kind in ("two", "sum")}
    ids.update({(k, name): arrival() for k in parts for name in ("two", "sum", "unit_two", "unit_sum")})

    def push(k, step, src, dst, columns, way, kind):
        send(6, ids[k, step, kind], line(src, k, step, columns), line(dst, k, step, columns), along(ORDERS[k][2], way))

    def push_plain(k, step):
        one, two = cut(0, width(k))
        push(k, step, send_plus, got_plus, two, 1, "sum")
        push(k, step, send_minus, got_minus, one, -1, "sum")

    def push_sums(k, step):
        one, two = cut(0, width(k))
        arrive(ids[k, step, "two"], line(got_plus, k, step))
        add_into(line(send_plus, k, step, one), line(got_two_plus, k, step, one))
        push(k, step, send_plus, got_plus, one, 1, "sum")
        add_into(line(send_minus, k, step, two), line(got_two_minus, k, step, two))
        push(k, step, send_minus, got_minus, two, -1, "sum")

    def push_line(k, src, dst, columns, way, kind):
        send(7, ids[k, kind], src.at[k, :, :, columns], dst.at[k, :, :, columns], along(ORDERS[k][1], way))

    def finish(k, step):
        one, two, full = halves(k)
        arrive(ids[k, step, "sum"], got_plus.at[k, 0:2, :, :, full])
        value = (line(total, k, step)[...] + line(got_plus, k, step)[...].astype(F32)
                 + line(got_minus, k, step)[...].astype(F32))
        if step == 2:
            line_two[k, :, :, full] = value.astype(BF16)
            push_line(k, line_two, line_got_two_plus, one, 1, "two")
            push_line(k, line_two, line_got_two_minus, two, -1, "two")
        elif step == 1:
            line_plus[k, :, :, full] = value.astype(BF16)
            push_line(k, line_plus, line_got_plus, two, 1, "sum")
        elif step == -1:
            line_minus[k, :, :, full] = value.astype(BF16)
            push_line(k, line_minus, line_got_minus, one, -1, "sum")
        else:
            line(total, k, 0)[...] = value

    def push_line_sums(k):
        one, two, full = halves(k)
        arrive(ids[k, "two"], line_got_plus.at[k, :, :, full])
        add_into(line_plus.at[k, :, :, one], line_got_two_plus.at[k, :, :, one])
        push_line(k, line_plus, line_got_plus, one, 1, "sum")
        add_into(line_minus.at[k, :, :, two], line_got_two_minus.at[k, :, :, two])
        push_line(k, line_minus, line_got_minus, two, -1, "sum")

    for k in parts:
        one, two = cut(0, width(k))
        terms(k, 2, fill(send_two, k))
        for step in (2, 1, -1, 0):
            push(k, step, send_two, got_two_plus, one, 1, "two")
            push(k, step, send_two, got_two_minus, two, -1, "two")
    for k in parts:
        terms(k, 1, fill(send_plus, k))
        terms(k, -1, fill(send_minus, k))
        push_plain(k, 2)
    for k in parts:
        terms(k, 0, fill(total, k))
    for step, later in ((2, 1), (1, -1), (-1, 0)):
        for k in parts:
            push_sums(k, step)
        for k in parts:
            push_plain(k, later)
    for k in parts:
        finish(k, 2)
    for k in parts:
        push_sums(k, 0)
    for step in (1, -1):
        for k in parts:
            finish(k, step)
    for k in parts:
        push_line_sums(k)
    for k in parts:
        finish(k, 0)

    def push_unit(k, src, dst, way, kind):
        full = halves(k)[2]
        send(8, ids[k, kind], src.at[k, :, full], dst.at[k, :, full], along(ORDERS[k][0], way))

    for k in parts:
        a = ORDERS[k][0]
        full = halves(k)[2]
        arrive(ids[k, "sum"], got_plus.at[k, 0:2, :, :, full])
        add_into(line(total, k, 0), line_got_plus.at[k, :, :, full], line_got_minus.at[k, :, :, full])
        whole = line(total, k, 0)
        unit_two[k, :, full] = whole.at[near(a, 2)][...].astype(BF16)
        push_unit(k, unit_two, unit_got_two, 1, "unit_two")
        unit_minus[k, :, full] = whole.at[near(a, -1)][...].astype(BF16)
        push_unit(k, unit_minus, unit_got_minus, -1, "unit_sum")
    for k in parts:
        a = ORDERS[k][0]
        full = halves(k)[2]
        arrive(ids[k, "unit_two"], unit_got_two.at[k, :, full])
        value = line(total, k, 0).at[near(a, 1)][...] + unit_got_two[k, :, full].astype(F32)
        unit_plus[k, :, full] = value.astype(BF16)
        push_unit(k, unit_plus, unit_got_plus, 1, "unit_sum")
    last = arrival()
    kept = []
    for k in parts:
        a = ORDERS[k][0]
        full = halves(k)[2]
        arrive(ids[k, "unit_sum"], got_plus.at[k, 0, 0:2, :, full])
        value = (line(total, k, 0).at[near(a, 0)][...] + unit_got_plus[k, :, full].astype(F32)
                 + unit_got_minus[k, :, full].astype(F32))
        value = stream[:, slice(*TERMS[k])] + value
        kept.append(jnp.where(first, value[0:4], value[4:8]))
        to_tp[:, slice(*TERMS[k])] = jnp.where(first, value[4:8], value[0:4]).astype(BF16)
    send(9, last, to_tp, from_tp, pair)
    for group, src in (
        (0, residual.at[:, 0:HALF]), (1, w_bytes), (2, d_bytes),
        (3, g.at[0:3, 0, 0]), (4, g.at[0:3, 0]), (5, g.at[0:3]),
        (6, g.at[0:3, :, :, :, 0:HALF]), (7, g.at[0:3, 0, :, :, 0:HALF]), (8, g.at[0:3, 0, 0, :, 0:HALF]),
    ):
        sent(group, src)
    arrive(last, from_tp)
    for k in parts:
        lo, hi = TERMS[k]
        theirs = from_tp[:, lo:hi].astype(F32)
        out[:, lo:hi] = jnp.where(first, kept[k], theirs)
        out[:, HALF + lo:HALF + hi] = jnp.where(first, theirs, kept[k])
    sent(9, to_tp)


def shards(
    queries, new_keys, token_values, key_cache, stored_values, cache_lengths, residual, norm_gain,
    active, gate_weight, up_weight, down_weight,
):
    vmem = pl.BlockSpec(memory_space=pltpu.VMEM)
    hbm = pl.BlockSpec(memory_space=pl.ANY)
    slab = (3, 4, 4, ROWS, 1408)
    rows = (3, 4, ROWS, 1408)
    unit = (3, ROWS, 1408)
    return pl.pallas_call(
        kernel,
        out_shape=jax.ShapeDtypeStruct((4, 8192), F32),
        in_specs=[pl.BlockSpec(memory_space=pltpu.SMEM)] + [vmem] * 6 + [hbm] * 5,
        out_specs=vmem,
        scratch_shapes=[
            pltpu.VMEM((ROWS, 256, 512), BF16),
            pltpu.VMEM((ROWS, 256, 512), BF16),
            pltpu.VMEM((2, HALF, 512), BF16),
            pltpu.VMEM((2, 256, HALF), BF16),
            pltpu.VMEM((4, 4, 4, ROWS, WIDTH), BF16),
            pltpu.VMEM((2, 4, 4, ROWS, 512), F32),
            pltpu.VMEM((2, 4, 4, ROWS, 256), BF16),
            pltpu.VMEM((ROWS, HALF), F32),
            pltpu.VMEM((4, 64, 256), F32),
            pltpu.VMEM((4, 64, 256), BF16),
            pltpu.VMEM((4, 64, 128), F32),
            pltpu.VMEM((4, HALF), BF16),
            pltpu.VMEM((4, HALF), BF16),
            pltpu.VMEM((4, HALF), BF16),
        ]
        + [pltpu.VMEM(slab, BF16)] * 7
        + [pltpu.VMEM(slab, F32)]
        + [pltpu.VMEM(rows, BF16)] * 7
        + [pltpu.VMEM(unit, BF16)] * 6
        + [
            pltpu.SemaphoreType.DMA((SENDS,)),
            pltpu.SemaphoreType.DMA((ARRIVALS,)),
            pltpu.SemaphoreType.DMA((FETCHES,)),
        ],
        compiler_params=pltpu.CompilerParams(
            collective_id=0, has_side_effects=True, vmem_limit_bytes=60 * 2**20),
    )(cache_lengths, queries, new_keys, token_values, residual, norm_gain.reshape(1, 8192), active,
      key_cache, stored_values, gate_weight, up_weight, down_weight).astype(BF16)


def solution(mesh):
    return jax.shard_map(
        shards,
        mesh=mesh,
        in_specs=(
            P(("sec", "dev"), "tp"),
            P(("sec", "dev"), "tp"),
            P(("sec", "dev"), "tp"),
            P(("sec", "dev"), None, "tp"),
            P(("sec", "dev"), None, "tp"),
            P(("sec", "dev")),
            P(("sec", "dev", "tp"), None),
            P(),
            P(("sec", "dev", "tp"), None),
            P(None, ("sec", "dev", "tp")),
            P(None, ("sec", "dev", "tp")),
            P(("sec", "dev", "tp"), None),
        ),
        out_specs=P(("sec", "dev", "tp"), None),
        check_vma=False,
    )
```

```python
import functools

import jax
import jax.numpy as jnp
from jax import lax
from jax.experimental import pallas as pl
from jax.experimental.pallas import tpu as pltpu
from jax.sharding import PartitionSpec as P

MESH = pl.DeviceIdType.MESH
EPSILON = 1e-05
F32 = jnp.float32
BF16 = jnp.bfloat16

ROWS = 8
HALF = 4096
WIDTH = HALF + 128
SPANS = ((0, 1408), (1408, 2816), (2816, 4224))
TERMS = ((0, 1408), (1408, 2816), (2816, 4096))
ORDERS = (("x", "y", "z"), ("y", "z", "x"), ("z", "x", "y"))
SENDS = 10
ARRIVALS = 139
FETCHES = 25


def cut(lo, hi):
    middle = lo + ((hi - lo) // 128 + 1) // 2 * 128
    return (lo, middle), (middle, hi)


def kernel(
    lengths_in, queries_in, new_keys_in, token_values_in, residual_in, gain_in, active_in,
    key_cache, stored_values, gate, up, down,
    out,
    lengths, queries, new_keys, token_values, residual, gain, active,
    keys, values, w, d, g, acc, hid, stream, scores, probs, blend, other_resid, to_tp, from_tp,
    send_two, send_plus, send_minus, got_two_plus, got_two_minus, got_plus, got_minus, total,
    line_two, line_plus, line_minus, line_got_two_plus, line_got_two_minus, line_got_plus, line_got_minus,
    unit_two, unit_plus, unit_minus, unit_got_two, unit_got_plus, unit_got_minus,
    send_sems, recv_sems, local_sems,
):
    sec, dev, tp = lax.axis_index("sec"), lax.axis_index("dev"), lax.axis_index("tp")
    core = lax.rem(dev, 2)
    here = {"x": lax.rem(dev // 2, 4), "y": sec * 2 + tp, "z": dev // 8}

    def device(x, y, z, core):
        return (y // 2, (z * 4 + x) * 2 + core, lax.rem(y, 2))

    def along(dim, step):
        at = dict(here)
        at[dim] = lax.rem(here[dim] + step + 4, 4)
        return device(at["x"], at["y"], at["z"], core)

    twin = device(here["x"], here["y"], here["z"], 1 - core)
    pair = (sec, dev, 1 - tp)

    used = []

    def arrival():
        used.append(None)
        return len(used) - 1

    def send(group, i, src, dst, target):
        pltpu.make_async_remote_copy(
            src_ref=src, dst_ref=dst, send_sem=send_sems.at[group], recv_sem=recv_sems.at[i],
            device_id=target, device_id_type=MESH,
        ).start()

    def arrive(i, dst):
        pltpu.make_async_remote_copy(
            src_ref=dst, dst_ref=dst, send_sem=send_sems.at[0], recv_sem=recv_sems.at[i],
            device_id=twin, device_id_type=MESH,
        ).wait_recv()

    def sent(group, src):
        pltpu.make_async_remote_copy(
            src_ref=src, dst_ref=src, send_sem=send_sems.at[group], recv_sem=recv_sems.at[0],
            device_id=twin, device_id_type=MESH,
        ).wait_send()

    def fetch(src, dst, i):
        copy = pltpu.make_async_copy(src, dst, local_sems.at[i])
        copy.start()
        return copy

    small = [fetch(src, dst, 18 + n) for n, (src, dst) in enumerate((
        (lengths_in, lengths), (queries_in, queries), (new_keys_in, new_keys), (token_values_in, token_values),
        (residual_in, residual), (gain_in, gain), (active_in, active)))]
    key_rows = [fetch(key_cache.at[r], keys.at[r], r) for r in range(ROWS)]
    value_rows = [fetch(stored_values.at[r], values.at[r], ROWS + r) for r in range(ROWS)]
    mine = pl.ds(pl.multiple_of(core * 128, 128), 128)
    mine_up = pl.ds(pl.multiple_of(256 + core * 128, 128), 128)
    pieces = []
    for t in range(2):
        rows = slice(t * HALF, (t + 1) * HALF)
        pieces.append((gate.at[rows, :], w.at[t, :, mine]))
        pieces.append((up.at[rows, :], w.at[t, :, mine_up]))
    for t in range(2):
        pieces.append((down.at[:, slice(t * HALF, (t + 1) * HALF)], d.at[t, mine, :]))
    for n, (src, dst) in enumerate(pieces):
        fetch(src, dst, 16 + n // 4)
    w_bytes, d_bytes = w.at[:, :, 0:256], d.at[:, 0:128, :]

    barrier = pltpu.get_barrier_semaphore()
    greeted = [twin] + [along(dim, step) for dim in ("x", "y", "z") for step in (1, -1)]
    for target in greeted:
        pl.semaphore_signal(barrier, inc=1, device_id=target, device_id_type=MESH)
    pl.semaphore_wait(barrier, len(greeted))

    theirs_half = pl.ds(pl.multiple_of((1 - tp) * HALF, 128), HALF)
    resid_id, w_id, d_id = arrival(), arrival(), arrival()
    send(0, resid_id, residual_in.at[:, theirs_half], other_resid, pair)
    for n, (src, dst) in enumerate(pieces):
        send(1 + n // 4, (w_id, d_id)[n // 4], src, dst, twin)

    for copy in small:
        copy.wait()

    first = tp == 0
    scale = 128 ** (-0.5)
    row_of = lax.rem(lax.broadcasted_iota(jnp.int32, (64, 1), 0), ROWS)
    limit = jnp.zeros((64, 1), jnp.int32)
    for r in range(ROWS):
        limit = jnp.where(row_of == r, lengths[r], limit)
    grouped = []
    for j in range(4):
        grouped.append(jnp.concatenate(
            [queries[:, (j * 8 + i) * 128:(j * 8 + i + 1) * 128].astype(F32) for i in range(8)], axis=0))
    for r in range(ROWS):
        key_rows[r].wait()
        for j in range(4):
            s = lax.dot_general(
                grouped[j].astype(BF16), keys[r, :, j * 128:(j + 1) * 128], (((1,), (1,)), ((), ())),
                preferred_element_type=F32)
            scores[j] = s if r == 0 else jnp.where(row_of == r, s, scores[j])
    column = lax.broadcasted_iota(jnp.int32, (64, 256), 1)
    fresh_probs = []
    for j in range(4):
        s = jnp.where(column < limit, scores[j] * scale, -1e30)
        fresh_key = jnp.concatenate([new_keys[:, j * 128:(j + 1) * 128].astype(F32)] * 8, axis=0)
        fresh = jnp.sum(grouped[j] * fresh_key, axis=1, keepdims=True) * scale
        highest = jnp.maximum(jnp.max(s, axis=1, keepdims=True), fresh)
        e = jnp.exp(s - highest)
        fresh_e = jnp.exp(fresh - highest)
        denominator = jnp.sum(e, axis=1, keepdims=True) + fresh_e
        probs[j] = (e / denominator).astype(BF16)
        fresh_probs.append((fresh_e / denominator).astype(BF16).astype(F32))
    for r in range(ROWS):
        value_rows[r].wait()
        for j in range(4):
            o = jnp.dot(probs[j], values[r, :, j * 128:(j + 1) * 128], preferred_element_type=F32)
            blend[j] = o if r == 0 else jnp.where(row_of == r, o, blend[j])

    lane = lax.broadcasted_iota(jnp.int32, (4, 128), 1)
    named = jnp.zeros((4, 128), F32)
    for k in range(16):
        named = jnp.where(active[:, k:k + 1] == lane, 1.0, named)

    arrive(resid_id, other_resid)
    me = (here["y"], here["z"], here["x"])
    squares = jnp.zeros((ROWS, 128), F32)
    for j in range(4):
        fresh_value = jnp.concatenate([token_values[:, j * 128:(j + 1) * 128].astype(F32)] * 8, axis=0)
        block = (blend[j] + fresh_probs[j] * fresh_value).astype(BF16).astype(F32)
        for i in range(8):
            lo = (j * 8 + i) * 128
            own = jnp.where(first, residual[:, lo:lo + 128], residual[:, HALF + lo:HALF + lo + 128]).astype(F32)
            other = other_resid[:, lo:lo + 128].astype(F32)
            resid = jnp.concatenate(
                [jnp.where(first, own, other), jnp.where(first, other, own)], axis=0)
            value = resid + block[i * 8:(i + 1) * 8]
            stream[:, lo:lo + 128] = value
            part = block[i * 8:(i + 1) * 8]
            to_tp[:, lo:lo + 128] = jnp.where(first, part[4:8], part[0:4]).astype(BF16)
            squares = squares + value * value
            factor = jnp.where(first, gain[:, lo:lo + 128], gain[:, HALF + lo:HALF + lo + 128])
            g[me + (slice(None), slice(lo, lo + 128))] = (value * factor).astype(BF16)
    sub8 = lax.broadcasted_iota(jnp.int32, (ROWS, 128), 0)
    lane8 = lax.broadcasted_iota(jnp.int32, (ROWS, 128), 1)
    row_sums = jnp.sum(squares, axis=1, keepdims=True)
    sums = jnp.sum(jnp.where(sub8 == lane8, row_sums, 0.0), axis=0, keepdims=True)
    sums_hi = sums.astype(BF16).astype(F32)
    sums_lo = sums - sums_hi
    lower = lax.broadcasted_iota(jnp.int32, (4, 128), 0)
    told = jnp.where(lower == 0, sums_hi, jnp.where(lower == 1, sums_lo, 0.0))
    extra = jnp.concatenate([jnp.where(first, named, told), jnp.where(first, told, named)], axis=0)
    g[me + (slice(None), slice(HALF, WIDTH))] = extra.astype(BF16)

    def spot(at, columns):
        index = tuple(at[dim] if dim in at else slice(None) for dim in ("y", "z", "x"))
        return g.at[index + (slice(None), slice(*columns))]

    def near(dim, step):
        return lax.rem(here[dim] + step + 4, 4)

    class Ring:
        def __init__(self, k, group, dim, fixed, far):
            self.columns, self.group, self.dim, self.fixed, self.far = SPANS[k], group, dim, fixed, far

        def region(self, step, columns):
            at = dict(self.fixed)
            at[self.dim] = near(self.dim, step)
            return spot(at, columns)

        def open(self):
            part = self.region(0, self.columns)
            self.plus, self.minus = arrival(), arrival()
            send(self.group, self.plus, part, part, along(self.dim, 1))
            send(self.group, self.minus, part, part, along(self.dim, -1))

        def relay(self):
            one, two = cut(*self.columns)
            arrive(self.plus, self.region(-1, self.columns))
            part = self.region(-1, one)
            send(self.group, self.far, part, part, along(self.dim, 1))
            arrive(self.minus, self.region(1, self.columns))
            part = self.region(1, two)
            send(self.group, self.far, part, part, along(self.dim, -1))

    parts = range(3)
    around = (0, 1, -1, 2)
    rings = []
    for k in parts:
        a, b, c = ORDERS[k]
        far = [arrival() for _ in range(3)]
        units = Ring(k, 3, a, {b: here[b], c: here[c]}, far[0])
        second = {step: Ring(k, 4, b, {a: near(a, step), c: here[c]}, far[1]) for step in around}
        third = {step: Ring(k, 5, c, {a: near(a, step), b: here[b]}, far[2]) for step in around}
        lines = {step: Ring(k, 5, c, {b: near(b, step)}, far[2]) for step in (1, -1, 2)}
        rings.append((units, second, third, lines))

    def close(k, phase):
        dims = ORDERS[k][:phase + 1]
        at = {dim: here[dim] for dim in ORDERS[k][phase + 1:]}
        at[dims[-1]] = near(dims[-1], 2)
        arrive(rings[k][phase].far if phase == 0 else rings[k][phase][0].far, spot(at, SPANS[k]))

    def multiply(k, step):
        lo, hi = SPANS[k][0], min(SPANS[k][1], HALF)
        c = ORDERS[k][2]
        at = near(c, step)
        columns = slice(lo, hi)
        n = hi - lo
        if c == "y":
            rows = g[at, :, :, :, columns].reshape(128, n)
            part = jnp.dot(rows, w[lax.rem(at, 2), columns, :], preferred_element_type=F32)
            acc[at // 2] += part.reshape(4, 4, ROWS, 512)
            return
        part = 0.0
        for t in range(2):
            if c == "z":
                rows = jnp.concatenate([g[y, at, :, :, columns].reshape(32, n) for y in (t, 2 + t)], axis=0)
            else:
                rows = jnp.concatenate([g[y, :, at, :, columns].reshape(32, n) for y in (t, 2 + t)], axis=0)
            part = part + jnp.dot(rows, w[t, columns, :], preferred_element_type=F32)
        part = part.reshape(2, 4, ROWS, 512)
        if c == "z":
            acc[:, at] += part
        else:
            acc[:, :, at] += part

    for phase in range(3):
        for k in parts:
            (rings[k][0] if phase == 0 else rings[k][phase][0]).open()
    context_id = arrival()
    send(9, context_id, to_tp, from_tp, pair)
    acc[...] = jnp.zeros_like(acc)
    for k in parts:
        rings[k][0].relay()
    for phase in (1, 2):
        for k in parts:
            rings[k][phase][1].open()
            rings[k][phase][-1].open()
    for k in parts:
        rings[k][1][0].relay()
    for k in parts:
        close(k, 0)
        rings[k][1][2].open()
    for k in parts:
        rings[k][2][2].open()
    for k in parts:
        rings[k][2][0].relay()
    for k in parts:
        rings[k][1][1].relay()
        rings[k][1][-1].relay()
    for k in parts:
        rings[k][1][2].relay()
    for k in parts:
        rings[k][3][1].open()
        rings[k][3][-1].open()
    for k in parts:
        rings[k][2][1].relay()
        rings[k][2][-1].relay()
    for k in parts:
        close(k, 1)
        rings[k][3][2].open()
    pltpu.make_async_copy(w_bytes, w_bytes, local_sems.at[16]).wait()
    arrive(w_id, w_bytes)
    for k in parts:
        multiply(k, 0)
        rings[k][2][2].relay()
    for step in (1, -1, 2):
        for k in parts:
            rings[k][3][step].relay()
    for k in parts:
        multiply(k, -1)
        multiply(k, 1)
    for k in parts:
        close(k, 2)
        multiply(k, 2)

    sub = lax.broadcasted_iota(jnp.int32, (32, ROWS, 128), 1)
    lanes = lax.broadcasted_iota(jnp.int32, (32, ROWS, 128), 2)
    extras = []
    for t in range(2):
        extras.append(jnp.concatenate(
            [g[y, :, :, :, HALF:WIDTH].astype(F32).reshape(16, ROWS, 128) for y in (t, 2 + t)], axis=0))
    names = jnp.where(sub < 4, extras[0], extras[1])
    bundle = sec * 64 + (dev - core) * 2 + tp
    wanted = [
        jnp.sum(jnp.where(lanes == bundle + 2 * i, names, 0.0), axis=2, keepdims=True).reshape(256, 1)
        for i in range(2)
    ]
    sums = (extras[0][:, 4:5] + extras[0][:, 5:6]) + (extras[1][:, 0:1] + extras[1][:, 1:2])
    mean = jnp.sum(jnp.where(lanes == sub, sums, 0.0), axis=2, keepdims=True).reshape(256, 1) / 8192.0
    inverse = lax.rsqrt(mean + EPSILON)
    gate_value = acc[:, :, :, :, 0:256].reshape(256, 256) * inverse
    up_value = acc[:, :, :, :, 256:512].reshape(256, 256) * inverse
    low = lax.broadcasted_iota(jnp.int32, (256, 256), 1) < 128
    hidden = jnp.maximum(gate_value, 0.0) * up_value * jnp.where(low, wanted[0], wanted[1])
    hid[...] = hidden.astype(BF16).reshape(2, 4, 4, ROWS, 256)

    pltpu.make_async_copy(d_bytes, d_bytes, local_sems.at[17]).wait()
    arrive(d_id, d_bytes)

    def terms(k, step, store):
        c = ORDERS[k][2]
        at = near(c, step)
        columns = slice(*TERMS[k])
        n = TERMS[k][1] - TERMS[k][0]
        if c == "y":
            rows = hid[at // 2].reshape(128, 256)
        else:
            rows = (hid[:, at] if c == "z" else hid[:, :, at]).reshape(64, 256)
        one, two = [
            jnp.dot(rows, d[t, :, columns], preferred_element_type=F32).reshape(-1, ROWS, n) for t in range(2)]
        above = lax.broadcasted_iota(jnp.int32, one.shape, 1) < 4
        crossed = pltpu.roll(jnp.where(above, two, one), 4, 1)
        if c == "y":
            even = lax.rem(at, 2) == 0
            value = jnp.where(above, jnp.where(even, one, crossed), jnp.where(even, crossed, two))
            store(slice(None), value.reshape(4, 4, ROWS, n))
            return
        for t, value in enumerate((jnp.where(above, one, crossed), jnp.where(above, crossed, two))):
            value = value.reshape(2, 4, ROWS, n)
            store(t, value[0])
            store(2 + t, value[1])

    def width(k):
        return TERMS[k][1] - TERMS[k][0]

    def line(ref, k, piece, columns=None):
        a, b, c = ORDERS[k]
        step, across = piece if isinstance(piece, tuple) else (piece, None)
        at = near(b, step)
        across = slice(None) if across is None else near(a, across)
        columns = slice(0, width(k)) if columns is None else slice(*columns)
        return ref.at[(k,) + ((at, across) if b == "y" else (across, at)) + (slice(None), columns)]

    def fill(ref, k):
        def store(y, value):
            if isinstance(y, slice):
                ref[k, :, :, :, 0:width(k)] = value.astype(ref.dtype)
            else:
                ref[k, y, :, :, 0:width(k)] = value.astype(ref.dtype)
        return store

    def add_into(ref, *others):
        value = ref[...].astype(F32)
        for other in others:
            value = value + other[...].astype(F32)
        ref[...] = value.astype(ref.dtype)

    def halves(k):
        one, two = cut(0, width(k))
        return slice(*one), slice(*two), slice(0, width(k))

    own = [(0, 2), (0, 1), (0, -1), (0, 0)]
    pieces = [2, 1, -1] + own
    ids = {(k, piece, kind): arrival() for k in parts for piece in pieces for kind in ("two", "sum")}
    ids.update({(k, name): arrival() for k in parts for name in ("two", "sum", "unit_two", "unit_sum")})

    def push(k, step, src, dst, columns, way, kind):
        send(6, ids[k, step, kind], line(src, k, step, columns), line(dst, k, step, columns), along(ORDERS[k][2], way))

    def push_plain(k, step):
        one, two = cut(0, width(k))
        push(k, step, send_plus, got_plus, two, 1, "sum")
        push(k, step, send_minus, got_minus, one, -1, "sum")

    def push_sums(k, step):
        one, two = cut(0, width(k))
        arrive(ids[k, step, "two"], line(got_plus, k, step))
        add_into(line(send_plus, k, step, one), line(got_two_plus, k, step, one))
        push(k, step, send_plus, got_plus, one, 1, "sum")
        add_into(line(send_minus, k, step, two), line(got_two_minus, k, step, two))
        push(k, step, send_minus, got_minus, two, -1, "sum")

    def push_line(k, src, dst, columns, way, kind):
        send(7, ids[k, kind], src.at[k, :, :, columns], dst.at[k, :, :, columns], along(ORDERS[k][1], way))

    def finish(k, step):
        one, two, full = halves(k)
        single = isinstance(step, tuple)
        arrive(ids[k, step, "sum"], got_plus.at[(k,) + ((0,) if single else ()) + (slice(0, 2),) + ((slice(None),) * (1 if single else 2)) + (full,)])
        value = (line(total, k, step)[...] + line(got_plus, k, step)[...].astype(F32)
                 + line(got_minus, k, step)[...].astype(F32))
        if step == 2:
            line_two[k, :, :, full] = value.astype(BF16)
            push_line(k, line_two, line_got_two_plus, one, 1, "two")
            push_line(k, line_two, line_got_two_minus, two, -1, "two")
        elif step == 1:
            line_plus[k, :, :, full] = value.astype(BF16)
            push_line(k, line_plus, line_got_plus, two, 1, "sum")
        elif step == -1:
            line_minus[k, :, :, full] = value.astype(BF16)
            push_line(k, line_minus, line_got_minus, one, -1, "sum")
        else:
            line(total, k, step)[...] = value

    def push_line_sums(k):
        one, two, full = halves(k)
        arrive(ids[k, "two"], line_got_plus.at[k, :, :, full])
        add_into(line_plus.at[k, :, :, one], line_got_two_plus.at[k, :, :, one])
        push_line(k, line_plus, line_got_plus, one, 1, "sum")
        add_into(line_minus.at[k, :, :, two], line_got_two_minus.at[k, :, :, two])
        push_line(k, line_minus, line_got_minus, two, -1, "sum")

    for k in parts:
        one, two = cut(0, width(k))
        terms(k, 2, fill(send_two, k))
        for step in pieces:
            push(k, step, send_two, got_two_plus, one, 1, "two")
            push(k, step, send_two, got_two_minus, two, -1, "two")
    for k in parts:
        terms(k, 1, fill(send_plus, k))
        terms(k, -1, fill(send_minus, k))
        push_plain(k, 2)
    for k in parts:
        terms(k, 0, fill(total, k))
    for now, later in (([2], [1]), ([1], [-1]), ([-1], own[:2])):
        for k in parts:
            for piece in now:
                push_sums(k, piece)
        for k in parts:
            for piece in later:
                push_plain(k, piece)
    for k in parts:
        finish(k, 2)
    for k in parts:
        push_sums(k, own[0])
        push_sums(k, own[1])
    for k in parts:
        push_plain(k, own[2])
        push_plain(k, own[3])
    for k in parts:
        finish(k, 1)
    for k in parts:
        push_sums(k, own[2])
        push_sums(k, own[3])
    for k in parts:
        finish(k, -1)
    for k in parts:
        push_line_sums(k)

    def push_unit(k, src, dst, way, kind):
        full = halves(k)[2]
        send(8, ids[k, kind], src.at[k, :, full], dst.at[k, :, full], along(ORDERS[k][0], way))

    def unit_sum(k, piece):
        a = ORDERS[k][0]
        full = halves(k)[2]
        finish(k, piece)
        at = near(a, piece[1])
        return (line(total, k, piece)[...] + line_got_plus[k, at, :, full].astype(F32)
                + line_got_minus[k, at, :, full].astype(F32))

    for k in parts:
        full = halves(k)[2]
        arrive(ids[k, "sum"], got_plus.at[k, 0:2, :, :, full])
        unit_two[k, :, full] = unit_sum(k, own[0]).astype(BF16)
        push_unit(k, unit_two, unit_got_two, 1, "unit_two")
    for k in parts:
        full = halves(k)[2]
        value = unit_sum(k, own[1])
        arrive(ids[k, "unit_two"], unit_got_two.at[k, :, full])
        unit_plus[k, :, full] = (value + unit_got_two[k, :, full].astype(F32)).astype(BF16)
        push_unit(k, unit_plus, unit_got_plus, 1, "unit_sum")
        unit_minus[k, :, full] = unit_sum(k, own[2]).astype(BF16)
        push_unit(k, unit_minus, unit_got_minus, -1, "unit_sum")
    arrive(context_id, from_tp)
    sums = [unit_sum(k, own[3]) for k in parts]
    for group, src in (
        (0, residual.at[:, 0:HALF]), (1, w_bytes), (2, d_bytes),
        (3, g.at[0:3, 0, 0]), (4, g.at[0:3, 0]), (5, g.at[0:3]), (9, to_tp),
        (6, g.at[0:3, :, :, :, 0:HALF]), (7, g.at[0:3, 0, :, :, 0:HALF]),
    ):
        sent(group, src)
    for k in parts:
        lo, hi = TERMS[k]
        full = halves(k)[2]
        ours = jnp.where(first, stream[0:4, lo:hi], stream[4:8, lo:hi])
        theirs = jnp.where(first, residual[:, HALF + lo:HALF + hi], residual[:, lo:hi]).astype(F32)
        theirs = theirs + from_tp[:, lo:hi].astype(F32)
        arrive(ids[k, "unit_sum"], got_plus.at[k, 0, 0:2, :, full])
        value = sums[k] + unit_got_plus[k, :, full].astype(F32) + unit_got_minus[k, :, full].astype(F32)
        out[:, lo:hi] = value[0:4] + jnp.where(first, ours, theirs)
        out[:, HALF + lo:HALF + hi] = value[4:8] + jnp.where(first, theirs, ours)
    sent(8, g.at[0:3, 0, 0, :, 0:HALF])


def shards(
    queries, new_keys, token_values, key_cache, stored_values, cache_lengths, residual, norm_gain,
    active, gate_weight, up_weight, down_weight,
):
    vmem = pl.BlockSpec(memory_space=pltpu.VMEM)
    hbm = pl.BlockSpec(memory_space=pltpu.HBM)
    slab = (3, 4, 4, ROWS, 1408)
    rows = (3, 4, ROWS, 1408)
    unit = (3, ROWS, 1408)
    return pl.pallas_call(
        kernel,
        out_shape=jax.ShapeDtypeStruct((4, 8192), F32),
        in_specs=[hbm] * 12,
        out_specs=vmem,
        scratch_shapes=[
            pltpu.SMEM((ROWS,), jnp.int32),
            pltpu.VMEM((ROWS, HALF), BF16),
            pltpu.VMEM((ROWS, 512), BF16),
            pltpu.VMEM((ROWS, 512), BF16),
            pltpu.VMEM((4, 8192), BF16),
            pltpu.VMEM((1, 8192), F32),
            pltpu.VMEM((4, 16), jnp.int32),
            pltpu.VMEM((ROWS, 256, 512), BF16),
            pltpu.VMEM((ROWS, 256, 512), BF16),
            pltpu.VMEM((2, HALF, 512), BF16),
            pltpu.VMEM((2, 256, HALF), BF16),
            pltpu.VMEM((4, 4, 4, ROWS, WIDTH), BF16),
            pltpu.VMEM((2, 4, 4, ROWS, 512), F32),
            pltpu.VMEM((2, 4, 4, ROWS, 256), BF16),
            pltpu.VMEM((ROWS, HALF), F32),
            pltpu.VMEM((4, 64, 256), F32),
            pltpu.VMEM((4, 64, 256), BF16),
            pltpu.VMEM((4, 64, 128), F32),
            pltpu.VMEM((4, HALF), BF16),
            pltpu.VMEM((4, HALF), BF16),
            pltpu.VMEM((4, HALF), BF16),
        ]
        + [pltpu.VMEM(slab, BF16)] * 7
        + [pltpu.VMEM(slab, F32)]
        + [pltpu.VMEM(rows, BF16)] * 7
        + [pltpu.VMEM(unit, BF16)] * 6
        + [
            pltpu.SemaphoreType.DMA((SENDS,)),
            pltpu.SemaphoreType.DMA((ARRIVALS,)),
            pltpu.SemaphoreType.DMA((FETCHES,)),
        ],
        compiler_params=pltpu.CompilerParams(
            collective_id=0, has_side_effects=True, vmem_limit_bytes=48 * 2**20),
    )(*[pltpu.with_memory_space_constraint(array, pltpu.HBM) for array in (
        cache_lengths, queries, new_keys, token_values, residual, norm_gain.reshape(1, 8192), active,
        key_cache, stored_values, gate_weight, up_weight, down_weight)]).astype(BF16)


def solution(mesh):
    return jax.shard_map(
        shards,
        mesh=mesh,
        in_specs=(
            P(("sec", "dev"), "tp"),
            P(("sec", "dev"), "tp"),
            P(("sec", "dev"), "tp"),
            P(("sec", "dev"), None, "tp"),
            P(("sec", "dev"), None, "tp"),
            P(("sec", "dev")),
            P(("sec", "dev", "tp"), None),
            P(),
            P(("sec", "dev", "tp"), None),
            P(None, ("sec", "dev", "tp")),
            P(None, ("sec", "dev", "tp")),
            P(("sec", "dev", "tp"), None),
        ),
        out_specs=P(("sec", "dev", "tp"), None),
        check_vma=False,
    )
```

```python
import functools

import jax
import jax.numpy as jnp
from jax import lax
from jax.experimental import pallas as pl
from jax.experimental.pallas import tpu as pltpu
from jax.sharding import PartitionSpec as P

MESH = pl.DeviceIdType.MESH
EPSILON = 1e-05
F32 = jnp.float32
BF16 = jnp.bfloat16

ROWS = 8
HALF = 4096
WIDTH = HALF + 128
SPANS = ((0, 1408), (1408, 2816), (2816, 4224))
TERMS = ((0, 1408), (1408, 2816), (2816, 4096))
ORDERS = (("x", "y", "z"), ("y", "z", "x"), ("z", "x", "y"))
SENDS = 10
ARRIVALS = 139
FETCHES = 25


def cut(lo, hi):
    middle = lo + ((hi - lo) // 128 + 1) // 2 * 128
    return (lo, middle), (middle, hi)


def kernel(
    lengths_in, queries_in, new_keys_in, token_values_in, residual_in, gain_in, active_in,
    key_cache, stored_values, gate, up, down,
    out,
    lengths, queries, new_keys, token_values, residual, gain, active,
    keys, values, w, d, g, acc, hid, stream, scores, probs, blend, other_resid, to_tp, from_tp,
    send_two, send_plus, send_minus, got_two_plus, got_two_minus, got_plus, got_minus, total,
    line_two, line_plus, line_minus, line_got_two_plus, line_got_two_minus, line_got_plus, line_got_minus,
    unit_two, unit_plus, unit_minus, unit_got_two, unit_got_plus, unit_got_minus,
    send_sems, recv_sems, local_sems,
):
    sec, dev, tp = lax.axis_index("sec"), lax.axis_index("dev"), lax.axis_index("tp")
    core = lax.rem(dev, 2)
    here = {"x": lax.rem(dev // 2, 4), "y": sec * 2 + tp, "z": dev // 8}

    def device(x, y, z, core):
        return (y // 2, (z * 4 + x) * 2 + core, lax.rem(y, 2))

    def along(dim, step):
        at = dict(here)
        at[dim] = lax.rem(here[dim] + step + 4, 4)
        return device(at["x"], at["y"], at["z"], core)

    twin = device(here["x"], here["y"], here["z"], 1 - core)
    pair = (sec, dev, 1 - tp)

    used = []

    def arrival():
        used.append(None)
        return len(used) - 1

    def send(group, i, src, dst, target):
        pltpu.make_async_remote_copy(
            src_ref=src, dst_ref=dst, send_sem=send_sems.at[group], recv_sem=recv_sems.at[i],
            device_id=target, device_id_type=MESH,
        ).start()

    def arrive(i, dst):
        pltpu.make_async_remote_copy(
            src_ref=dst, dst_ref=dst, send_sem=send_sems.at[0], recv_sem=recv_sems.at[i],
            device_id=twin, device_id_type=MESH,
        ).wait_recv()

    def sent(group, src):
        pltpu.make_async_remote_copy(
            src_ref=src, dst_ref=src, send_sem=send_sems.at[group], recv_sem=recv_sems.at[0],
            device_id=twin, device_id_type=MESH,
        ).wait_send()

    def fetch(src, dst, i):
        copy = pltpu.make_async_copy(src, dst, local_sems.at[i])
        copy.start()
        return copy

    small = [fetch(src, dst, 18 + n) for n, (src, dst) in enumerate((
        (lengths_in, lengths), (queries_in, queries), (new_keys_in, new_keys), (token_values_in, token_values),
        (residual_in, residual), (gain_in, gain), (active_in, active)))]
    key_rows = [fetch(key_cache.at[r], keys.at[r], r) for r in range(ROWS)]
    value_rows = [fetch(stored_values.at[r], values.at[r], ROWS + r) for r in range(ROWS)]
    mine = pl.ds(pl.multiple_of(core * 128, 128), 128)
    mine_up = pl.ds(pl.multiple_of(256 + core * 128, 128), 128)
    pieces = []
    for t in range(2):
        rows = slice(t * HALF, (t + 1) * HALF)
        pieces.append((gate.at[rows, :], w.at[t, :, mine]))
        pieces.append((up.at[rows, :], w.at[t, :, mine_up]))
    for t in range(2):
        pieces.append((down.at[:, slice(t * HALF, (t + 1) * HALF)], d.at[t, mine, :]))
    for n, (src, dst) in enumerate(pieces):
        fetch(src, dst, 16 + n // 4)
    w_bytes, d_bytes = w.at[:, :, 0:256], d.at[:, 0:128, :]

    barrier = pltpu.get_barrier_semaphore()
    greeted = [twin] + [along(dim, step) for dim in ("x", "y", "z") for step in (1, -1)]
    for target in greeted:
        pl.semaphore_signal(barrier, inc=1, device_id=target, device_id_type=MESH)
    pl.semaphore_wait(barrier, len(greeted))

    theirs_half = pl.ds(pl.multiple_of((1 - tp) * HALF, 128), HALF)
    resid_id, w_id, d_id = arrival(), arrival(), arrival()
    send(0, resid_id, residual_in.at[:, theirs_half], other_resid, pair)
    for n, (src, dst) in enumerate(pieces):
        send(1 + n // 4, (w_id, d_id)[n // 4], src, dst, twin)

    for copy in small:
        copy.wait()

    first = tp == 0
    scale = 128 ** (-0.5)
    row_of = lax.rem(lax.broadcasted_iota(jnp.int32, (64, 1), 0), ROWS)
    limit = jnp.zeros((64, 1), jnp.int32)
    for r in range(ROWS):
        limit = jnp.where(row_of == r, lengths[r], limit)
    grouped = []
    for j in range(4):
        grouped.append(jnp.concatenate(
            [queries[:, (j * 8 + i) * 128:(j * 8 + i + 1) * 128].astype(F32) for i in range(8)], axis=0))
    masks = [jnp.broadcast_to(jnp.where(row_of == r, 1.0, 0.0), (64, 128)).astype(BF16) for r in range(ROWS)]
    for part in (range(0, 4), range(4, 8)):
        for r in part:
            key_rows[r].wait()
        for j in range(4):
            asked = grouped[j].astype(BF16)
            s = lax.dot_general(
                jnp.concatenate([asked * masks[r] for r in part], axis=1),
                jnp.concatenate([keys[r, :, j * 128:(j + 1) * 128] for r in part], axis=1),
                (((1,), (1,)), ((), ())), preferred_element_type=F32)
            scores[j] = s if part[0] == 0 else scores[j] + s
    column = lax.broadcasted_iota(jnp.int32, (64, 256), 1)
    fresh_probs = []
    for j in range(4):
        s = jnp.where(column < limit, scores[j] * scale, -1e30)
        fresh_key = jnp.concatenate([new_keys[:, j * 128:(j + 1) * 128].astype(F32)] * 8, axis=0)
        fresh = jnp.sum(grouped[j] * fresh_key, axis=1, keepdims=True) * scale
        highest = jnp.maximum(jnp.max(s, axis=1, keepdims=True), fresh)
        e = jnp.exp(s - highest)
        fresh_e = jnp.exp(fresh - highest)
        denominator = jnp.sum(e, axis=1, keepdims=True) + fresh_e
        share = 1.0 / denominator
        probs[j] = (e * share).astype(BF16)
        fresh_probs.append((fresh_e * share).astype(BF16).astype(F32))
    for r in range(ROWS):
        value_rows[r].wait()
    for j in range(4):
        shares = probs[j]
        blend[j] = jnp.dot(
            jnp.concatenate([shares * jnp.concatenate([masks[r]] * 2, axis=1) for r in range(ROWS)], axis=1),
            jnp.concatenate([values[r, :, j * 128:(j + 1) * 128] for r in range(ROWS)], axis=0),
            preferred_element_type=F32)

    lane = lax.broadcasted_iota(jnp.int32, (4, 128), 1)
    named = jnp.zeros((4, 128), F32)
    for k in range(16):
        named = jnp.where(active[:, k:k + 1] == lane, 1.0, named)

    arrive(resid_id, other_resid)
    me = (here["y"], here["z"], here["x"])
    squares = jnp.zeros((ROWS, 128), F32)
    for j in range(4):
        fresh_value = jnp.concatenate([token_values[:, j * 128:(j + 1) * 128].astype(F32)] * 8, axis=0)
        block = (blend[j] + fresh_probs[j] * fresh_value).astype(BF16).astype(F32)
        for i in range(8):
            lo = (j * 8 + i) * 128
            own = jnp.where(first, residual[:, lo:lo + 128], residual[:, HALF + lo:HALF + lo + 128]).astype(F32)
            other = other_resid[:, lo:lo + 128].astype(F32)
            resid = jnp.concatenate(
                [jnp.where(first, own, other), jnp.where(first, other, own)], axis=0)
            value = resid + block[i * 8:(i + 1) * 8]
            stream[:, lo:lo + 128] = value
            part = block[i * 8:(i + 1) * 8]
            to_tp[:, lo:lo + 128] = jnp.where(first, part[4:8], part[0:4]).astype(BF16)
            squares = squares + value * value
            factor = jnp.where(first, gain[:, lo:lo + 128], gain[:, HALF + lo:HALF + lo + 128])
            g[me + (slice(None), slice(lo, lo + 128))] = (value * factor).astype(BF16)
    sub8 = lax.broadcasted_iota(jnp.int32, (ROWS, 128), 0)
    lane8 = lax.broadcasted_iota(jnp.int32, (ROWS, 128), 1)
    row_sums = jnp.sum(squares, axis=1, keepdims=True)
    sums = jnp.sum(jnp.where(sub8 == lane8, row_sums, 0.0), axis=0, keepdims=True)
    sums_hi = sums.astype(BF16).astype(F32)
    sums_lo = sums - sums_hi
    lower = lax.broadcasted_iota(jnp.int32, (4, 128), 0)
    told = jnp.where(lower == 0, sums_hi, jnp.where(lower == 1, sums_lo, 0.0))
    extra = jnp.concatenate([jnp.where(first, named, told), jnp.where(first, told, named)], axis=0)
    g[me + (slice(None), slice(HALF, WIDTH))] = extra.astype(BF16)

    def spot(at, columns):
        index = tuple(at[dim] if dim in at else slice(None) for dim in ("y", "z", "x"))
        return g.at[index + (slice(None), slice(*columns))]

    def near(dim, step):
        return lax.rem(here[dim] + step + 4, 4)

    class Ring:
        def __init__(self, k, group, dim, fixed, far):
            self.columns, self.group, self.dim, self.fixed, self.far = SPANS[k], group, dim, fixed, far

        def region(self, step, columns):
            at = dict(self.fixed)
            at[self.dim] = near(self.dim, step)
            return spot(at, columns)

        def open(self):
            part = self.region(0, self.columns)
            self.plus, self.minus = arrival(), arrival()
            send(self.group, self.plus, part, part, along(self.dim, 1))
            send(self.group, self.minus, part, part, along(self.dim, -1))

        def relay(self):
            one, two = cut(*self.columns)
            arrive(self.plus, self.region(-1, self.columns))
            part = self.region(-1, one)
            send(self.group, self.far, part, part, along(self.dim, 1))
            arrive(self.minus, self.region(1, self.columns))
            part = self.region(1, two)
            send(self.group, self.far, part, part, along(self.dim, -1))

    parts = range(3)
    around = (0, 1, -1, 2)
    rings = []
    for k in parts:
        a, b, c = ORDERS[k]
        far = [arrival() for _ in range(3)]
        units = Ring(k, 3, a, {b: here[b], c: here[c]}, far[0])
        second = {step: Ring(k, 4, b, {a: near(a, step), c: here[c]}, far[1]) for step in around}
        third = {step: Ring(k, 5, c, {a: near(a, step), b: here[b]}, far[2]) for step in around}
        lines = {step: Ring(k, 5, c, {b: near(b, step)}, far[2]) for step in (1, -1, 2)}
        rings.append((units, second, third, lines))

    def close(k, phase):
        dims = ORDERS[k][:phase + 1]
        at = {dim: here[dim] for dim in ORDERS[k][phase + 1:]}
        at[dims[-1]] = near(dims[-1], 2)
        arrive(rings[k][phase].far if phase == 0 else rings[k][phase][0].far, spot(at, SPANS[k]))

    def multiply(k, step):
        lo, hi = SPANS[k][0], min(SPANS[k][1], HALF)
        c = ORDERS[k][2]
        at = near(c, step)
        columns = slice(lo, hi)
        n = hi - lo
        if c == "y":
            rows = g[at, :, :, :, columns].reshape(128, n)
            part = jnp.dot(rows, w[lax.rem(at, 2), columns, :], preferred_element_type=F32)
            acc[at // 2] += part.reshape(4, 4, ROWS, 512)
            return
        part = 0.0
        for t in range(2):
            if c == "z":
                rows = jnp.concatenate([g[y, at, :, :, columns].reshape(32, n) for y in (t, 2 + t)], axis=0)
            else:
                rows = jnp.concatenate([g[y, :, at, :, columns].reshape(32, n) for y in (t, 2 + t)], axis=0)
            part = part + jnp.dot(rows, w[t, columns, :], preferred_element_type=F32)
        part = part.reshape(2, 4, ROWS, 512)
        if c == "z":
            acc[:, at] += part
        else:
            acc[:, :, at] += part

    for phase in range(3):
        for k in parts:
            (rings[k][0] if phase == 0 else rings[k][phase][0]).open()
    context_id = arrival()
    send(9, context_id, to_tp, from_tp, pair)
    acc[...] = jnp.zeros_like(acc)
    for k in parts:
        rings[k][0].relay()
    for phase in (1, 2):
        for k in parts:
            rings[k][phase][1].open()
            rings[k][phase][-1].open()
    for k in parts:
        rings[k][1][0].relay()
    for k in parts:
        close(k, 0)
        rings[k][1][2].open()
    for k in parts:
        rings[k][2][2].open()
    for k in parts:
        rings[k][2][0].relay()
    for k in parts:
        rings[k][1][1].relay()
        rings[k][1][-1].relay()
    for k in parts:
        rings[k][1][2].relay()
    for k in parts:
        rings[k][3][1].open()
        rings[k][3][-1].open()
    for k in parts:
        rings[k][2][1].relay()
        rings[k][2][-1].relay()
    for k in parts:
        close(k, 1)
        rings[k][3][2].open()
    pltpu.make_async_copy(w_bytes, w_bytes, local_sems.at[16]).wait()
    arrive(w_id, w_bytes)
    for k in parts:
        multiply(k, 0)
        rings[k][2][2].relay()
    for step in (1, -1, 2):
        for k in parts:
            rings[k][3][step].relay()
    for k in parts:
        multiply(k, -1)
        multiply(k, 1)
    for k in parts:
        close(k, 2)
        multiply(k, 2)

    sub = lax.broadcasted_iota(jnp.int32, (32, ROWS, 128), 1)
    lanes = lax.broadcasted_iota(jnp.int32, (32, ROWS, 128), 2)
    extras = []
    for t in range(2):
        extras.append(jnp.concatenate(
            [g[y, :, :, :, HALF:WIDTH].astype(F32).reshape(16, ROWS, 128) for y in (t, 2 + t)], axis=0))
    names = jnp.where(sub < 4, extras[0], extras[1])
    bundle = sec * 64 + (dev - core) * 2 + tp
    wanted = [
        jnp.sum(jnp.where(lanes == bundle + 2 * i, names, 0.0), axis=2, keepdims=True).reshape(256, 1)
        for i in range(2)
    ]
    sums = (extras[0][:, 4:5] + extras[0][:, 5:6]) + (extras[1][:, 0:1] + extras[1][:, 1:2])
    mean = jnp.sum(jnp.where(lanes == sub, sums, 0.0), axis=2, keepdims=True).reshape(256, 1) / 8192.0
    inverse = lax.rsqrt(mean + EPSILON)
    gate_value = acc[:, :, :, :, 0:256].reshape(256, 256) * inverse
    up_value = acc[:, :, :, :, 256:512].reshape(256, 256) * inverse
    low = lax.broadcasted_iota(jnp.int32, (256, 256), 1) < 128
    hidden = jnp.maximum(gate_value, 0.0) * up_value * jnp.where(low, wanted[0], wanted[1])
    hid[...] = hidden.astype(BF16).reshape(2, 4, 4, ROWS, 256)

    pltpu.make_async_copy(d_bytes, d_bytes, local_sems.at[17]).wait()
    arrive(d_id, d_bytes)

    def terms(k, step, store):
        c = ORDERS[k][2]
        at = near(c, step)
        columns = slice(*TERMS[k])
        n = TERMS[k][1] - TERMS[k][0]
        if c == "y":
            rows = hid[at // 2].reshape(128, 256)
        else:
            rows = (hid[:, at] if c == "z" else hid[:, :, at]).reshape(64, 256)
        one, two = [
            jnp.dot(rows, d[t, :, columns], preferred_element_type=F32).reshape(-1, ROWS, n) for t in range(2)]
        above = lax.broadcasted_iota(jnp.int32, one.shape, 1) < 4
        crossed = pltpu.roll(jnp.where(above, two, one), 4, 1)
        if c == "y":
            even = lax.rem(at, 2) == 0
            value = jnp.where(above, jnp.where(even, one, crossed), jnp.where(even, crossed, two))
            store(slice(None), value.reshape(4, 4, ROWS, n))
            return
        for t, value in enumerate((jnp.where(above, one, crossed), jnp.where(above, crossed, two))):
            value = value.reshape(2, 4, ROWS, n)
            store(t, value[0])
            store(2 + t, value[1])

    def width(k):
        return TERMS[k][1] - TERMS[k][0]

    def line(ref, k, piece, columns=None):
        a, b, c = ORDERS[k]
        step, across = piece if isinstance(piece, tuple) else (piece, None)
        at = near(b, step)
        across = slice(None) if across is None else near(a, across)
        columns = slice(0, width(k)) if columns is None else slice(*columns)
        return ref.at[(k,) + ((at, across) if b == "y" else (across, at)) + (slice(None), columns)]

    def fill(ref, k):
        def store(y, value):
            if isinstance(y, slice):
                ref[k, :, :, :, 0:width(k)] = value.astype(ref.dtype)
            else:
                ref[k, y, :, :, 0:width(k)] = value.astype(ref.dtype)
        return store

    def add_into(ref, *others):
        value = ref[...].astype(F32)
        for other in others:
            value = value + other[...].astype(F32)
        ref[...] = value.astype(ref.dtype)

    def halves(k):
        one, two = cut(0, width(k))
        return slice(*one), slice(*two), slice(0, width(k))

    own = [(0, 2), (0, 1), (0, -1), (0, 0)]
    pieces = [2, 1, -1] + own
    ids = {(k, piece, kind): arrival() for k in parts for piece in pieces for kind in ("two", "sum")}
    ids.update({(k, name): arrival() for k in parts for name in ("two", "sum", "unit_two", "unit_sum")})

    def push(k, step, src, dst, columns, way, kind):
        send(6, ids[k, step, kind], line(src, k, step, columns), line(dst, k, step, columns), along(ORDERS[k][2], way))

    def push_plain(k, step):
        one, two = cut(0, width(k))
        push(k, step, send_plus, got_plus, two, 1, "sum")
        push(k, step, send_minus, got_minus, one, -1, "sum")

    def push_sums(k, step):
        one, two = cut(0, width(k))
        arrive(ids[k, step, "two"], line(got_plus, k, step))
        add_into(line(send_plus, k, step, one), line(got_two_plus, k, step, one))
        push(k, step, send_plus, got_plus, one, 1, "sum")
        add_into(line(send_minus, k, step, two), line(got_two_minus, k, step, two))
        push(k, step, send_minus, got_minus, two, -1, "sum")

    def push_line(k, src, dst, columns, way, kind):
        send(7, ids[k, kind], src.at[k, :, :, columns], dst.at[k, :, :, columns], along(ORDERS[k][1], way))

    def finish(k, step):
        one, two, full = halves(k)
        single = isinstance(step, tuple)
        arrive(ids[k, step, "sum"], got_plus.at[(k,) + ((0,) if single else ()) + (slice(0, 2),) + ((slice(None),) * (1 if single else 2)) + (full,)])
        value = (line(total, k, step)[...] + line(got_plus, k, step)[...].astype(F32)
                 + line(got_minus, k, step)[...].astype(F32))
        if step == 2:
            line_two[k, :, :, full] = value.astype(BF16)
            push_line(k, line_two, line_got_two_plus, one, 1, "two")
            push_line(k, line_two, line_got_two_minus, two, -1, "two")
        elif step == 1:
            line_plus[k, :, :, full] = value.astype(BF16)
            push_line(k, line_plus, line_got_plus, two, 1, "sum")
        elif step == -1:
            line_minus[k, :, :, full] = value.astype(BF16)
            push_line(k, line_minus, line_got_minus, one, -1, "sum")
        else:
            line(total, k, step)[...] = value

    def push_line_sums(k):
        one, two, full = halves(k)
        arrive(ids[k, "two"], line_got_plus.at[k, :, :, full])
        add_into(line_plus.at[k, :, :, one], line_got_two_plus.at[k, :, :, one])
        push_line(k, line_plus, line_got_plus, one, 1, "sum")
        add_into(line_minus.at[k, :, :, two], line_got_two_minus.at[k, :, :, two])
        push_line(k, line_minus, line_got_minus, two, -1, "sum")

    for k in parts:
        one, two = cut(0, width(k))
        terms(k, 2, fill(send_two, k))
        for step in pieces:
            push(k, step, send_two, got_two_plus, one, 1, "two")
            push(k, step, send_two, got_two_minus, two, -1, "two")
    for k in parts:
        terms(k, 1, fill(send_plus, k))
        terms(k, -1, fill(send_minus, k))
        push_plain(k, 2)
    for k in parts:
        terms(k, 0, fill(total, k))
    for now, later in (([2], [1]), ([1], [-1]), ([-1], own[:2])):
        for k in parts:
            for piece in now:
                push_sums(k, piece)
        for k in parts:
            for piece in later:
                push_plain(k, piece)
    for k in parts:
        finish(k, 2)
    for k in parts:
        push_sums(k, own[0])
        push_sums(k, own[1])
    for k in parts:
        push_plain(k, own[2])
        push_plain(k, own[3])
    for k in parts:
        finish(k, 1)
    for k in parts:
        push_sums(k, own[2])
        push_sums(k, own[3])
    for k in parts:
        finish(k, -1)
    for k in parts:
        push_line_sums(k)

    def push_unit(k, src, dst, way, kind):
        full = halves(k)[2]
        send(8, ids[k, kind], src.at[k, :, full], dst.at[k, :, full], along(ORDERS[k][0], way))

    def unit_sum(k, piece):
        a = ORDERS[k][0]
        full = halves(k)[2]
        finish(k, piece)
        at = near(a, piece[1])
        return (line(total, k, piece)[...] + line_got_plus[k, at, :, full].astype(F32)
                + line_got_minus[k, at, :, full].astype(F32))

    for k in parts:
        full = halves(k)[2]
        arrive(ids[k, "sum"], got_plus.at[k, 0:2, :, :, full])
        unit_two[k, :, full] = unit_sum(k, own[0]).astype(BF16)
        push_unit(k, unit_two, unit_got_two, 1, "unit_two")
    for k in parts:
        full = halves(k)[2]
        value = unit_sum(k, own[1])
        arrive(ids[k, "unit_two"], unit_got_two.at[k, :, full])
        unit_plus[k, :, full] = (value + unit_got_two[k, :, full].astype(F32)).astype(BF16)
        push_unit(k, unit_plus, unit_got_plus, 1, "unit_sum")
        unit_minus[k, :, full] = unit_sum(k, own[2]).astype(BF16)
        push_unit(k, unit_minus, unit_got_minus, -1, "unit_sum")
    arrive(context_id, from_tp)
    sums = [unit_sum(k, own[3]) for k in parts]
    for group, src in (
        (0, residual.at[:, 0:HALF]), (1, w_bytes), (2, d_bytes),
        (3, g.at[0:3, 0, 0]), (4, g.at[0:3, 0]), (5, g.at[0:3]), (9, to_tp),
        (6, g.at[0:3, :, :, :, 0:HALF]), (7, g.at[0:3, 0, :, :, 0:HALF]),
    ):
        sent(group, src)
    for k in parts:
        lo, hi = TERMS[k]
        full = halves(k)[2]
        ours = jnp.where(first, stream[0:4, lo:hi], stream[4:8, lo:hi])
        theirs = jnp.where(first, residual[:, HALF + lo:HALF + hi], residual[:, lo:hi]).astype(F32)
        theirs = theirs + from_tp[:, lo:hi].astype(F32)
        arrive(ids[k, "unit_sum"], got_plus.at[k, 0, 0:2, :, full])
        value = sums[k] + unit_got_plus[k, :, full].astype(F32) + unit_got_minus[k, :, full].astype(F32)
        out[:, lo:hi] = value[0:4] + jnp.where(first, ours, theirs)
        out[:, HALF + lo:HALF + hi] = value[4:8] + jnp.where(first, theirs, ours)
    sent(8, g.at[0:3, 0, 0, :, 0:HALF])


def shards(
    queries, new_keys, token_values, key_cache, stored_values, cache_lengths, residual, norm_gain,
    active, gate_weight, up_weight, down_weight,
):
    vmem = pl.BlockSpec(memory_space=pltpu.VMEM)
    hbm = pl.BlockSpec(memory_space=pltpu.HBM)
    slab = (3, 4, 4, ROWS, 1408)
    rows = (3, 4, ROWS, 1408)
    unit = (3, ROWS, 1408)
    return pl.pallas_call(
        kernel,
        out_shape=jax.ShapeDtypeStruct((4, 8192), F32),
        in_specs=[hbm] * 12,
        out_specs=vmem,
        scratch_shapes=[
            pltpu.SMEM((ROWS,), jnp.int32),
            pltpu.VMEM((ROWS, HALF), BF16),
            pltpu.VMEM((ROWS, 512), BF16),
            pltpu.VMEM((ROWS, 512), BF16),
            pltpu.VMEM((4, 8192), BF16),
            pltpu.VMEM((1, 8192), F32),
            pltpu.VMEM((4, 16), jnp.int32),
            pltpu.VMEM((ROWS, 256, 512), BF16),
            pltpu.VMEM((ROWS, 256, 512), BF16),
            pltpu.VMEM((2, HALF, 512), BF16),
            pltpu.VMEM((2, 256, HALF), BF16),
            pltpu.VMEM((4, 4, 4, ROWS, WIDTH), BF16),
            pltpu.VMEM((2, 4, 4, ROWS, 512), F32),
            pltpu.VMEM((2, 4, 4, ROWS, 256), BF16),
            pltpu.VMEM((ROWS, HALF), F32),
            pltpu.VMEM((4, 64, 256), F32),
            pltpu.VMEM((4, 64, 256), BF16),
            pltpu.VMEM((4, 64, 128), F32),
            pltpu.VMEM((4, HALF), BF16),
            pltpu.VMEM((4, HALF), BF16),
            pltpu.VMEM((4, HALF), BF16),
        ]
        + [pltpu.VMEM(slab, BF16)] * 7
        + [pltpu.VMEM(slab, F32)]
        + [pltpu.VMEM(rows, BF16)] * 7
        + [pltpu.VMEM(unit, BF16)] * 6
        + [
            pltpu.SemaphoreType.DMA((SENDS,)),
            pltpu.SemaphoreType.DMA((ARRIVALS,)),
            pltpu.SemaphoreType.DMA((FETCHES,)),
        ],
        compiler_params=pltpu.CompilerParams(
            collective_id=0, has_side_effects=True, vmem_limit_bytes=48 * 2**20),
    )(*[pltpu.with_memory_space_constraint(array, pltpu.HBM) for array in (
        cache_lengths, queries, new_keys, token_values, residual, norm_gain.reshape(1, 8192), active,
        key_cache, stored_values, gate_weight, up_weight, down_weight)]).astype(BF16)


def solution(mesh):
    return jax.shard_map(
        shards,
        mesh=mesh,
        in_specs=(
            P(("sec", "dev"), "tp"),
            P(("sec", "dev"), "tp"),
            P(("sec", "dev"), "tp"),
            P(("sec", "dev"), None, "tp"),
            P(("sec", "dev"), None, "tp"),
            P(("sec", "dev")),
            P(("sec", "dev", "tp"), None),
            P(),
            P(("sec", "dev", "tp"), None),
            P(None, ("sec", "dev", "tp")),
            P(None, ("sec", "dev", "tp")),
            P(("sec", "dev", "tp"), None),
        ),
        out_specs=P(("sec", "dev", "tp"), None),
        check_vma=False,
    )
```
